32 devices in a mesh: band: 2 (over x), gx: 16 (over z, y, core).
Axes of the slice: x: 2, y: 2, z: 4, core: 2. Of those that a mesh axis runs over, the one named last changes fastest.
Arguments:
- slc_tiles: bfloat16 [64, 2, 64, 2048], P('gx', None, 'band'), parts along dimension 2, may hold values from -64 to 64
- look_weight: float32 [64, 2048], P('band'), parts along dimension 0, may hold values from 0.05 to 1
- pair_list: int32 [192, 2], replicated, may hold values from 0 to 63, as said below
Outputs:
- corrected: float32 [64, 64, 2048], P(None, 'band', 'gx'), parts along dimension 1
The draws below stay inside these ranges and needn't reach their ends.
There are 2 independent parts, one for each index of `band`. The reference program is written for one: setup_inputs(seed, part) draws one part's arguments, and reference() takes and returns one part's arrays. A program takes and returns all parts, laid end to end along the dimension named above; an argument that names none is the same for every part. Nothing has to cross between parts.
Inputs may be any that keep to these rules, and one draw needn't show every extreme that they name: `pair_list`: row p is a pair of date indices; with d = p // 12, the reference date lies in d * 4 to (d + 1) * 4 - 1 and the secondary date is 1 to 4 dates after it.
All inputs are finite; a program needn't handle non-finite values.
Results may differ from the reference program's by a relative error of at most 0.0071.
Values may be sent and summed in bfloat16 or wider, within the bound.
No kernel may reach another device: no remote copies, remote signals or barrier semaphores. Data moves between devices by JAX's collectives and lax.ppermute only.
A program may use at most 128 MiB of HBM per device.

```python
import math
import jax
import jax.numpy as jnp
from jax import lax

DATE_DEV = 4
ROWS = 32
LOOK = 9
DATES = 64
PAIR_DEV = 12
PAIRS = 192
COLS = 2048


def draw_slc_tiles(key, part):
    subkeys = jax.random.split(key, 10)
    col_coord = (2.0 * jnp.arange(COLS, dtype=jnp.float32) + 1.0) / COLS - 1.0
    date_index = jnp.arange(DATES, dtype=jnp.float32)[:, None, None]
    scatter_re = jax.random.normal(subkeys[0], (ROWS, COLS), jnp.float32)
    scatter_im = jax.random.normal(subkeys[1], (ROWS, COLS), jnp.float32)
    amplitude = jnp.exp(jax.random.uniform(subkeys[2], (ROWS, COLS), jnp.float32, -1.2, 1.2))
    noise_re = 0.4 * jax.random.normal(subkeys[8], (DATES, ROWS, COLS), jnp.float32)
    noise_im = 0.4 * jax.random.normal(subkeys[9], (DATES, ROWS, COLS), jnp.float32)
    offsets = jax.random.uniform(subkeys[3], (DATES, 1, 1), jnp.float32, -1.0, 1.0)
    slopes = jax.random.uniform(subkeys[4], (DATES, 1, 1), jnp.float32, -1.5, 1.5)
    motion = jax.random.uniform(subkeys[5], (ROWS, COLS), jnp.float32, -1.0, 1.0) * (2.0 / DATES)
    rough = 0.4 * jax.random.normal(subkeys[6], (DATES, ROWS, COLS), jnp.float32)
    phase = offsets + slopes * col_coord + motion * date_index + rough
    cosine = jnp.cos(phase)
    sine = jnp.sin(phase)
    real_part = amplitude * (scatter_re * cosine - scatter_im * sine) + noise_re
    imag_part = amplitude * (scatter_re * sine + scatter_im * cosine) + noise_im
    stacked = jnp.clip(jnp.stack([real_part, imag_part], axis=1), -64.0, 64.0)
    return stacked.astype(jnp.bfloat16)


def draw_pair_list(key, part):
    subkeys = jax.random.split(key, 2)
    row_index = jnp.arange(PAIRS, dtype=jnp.int32)
    first_date = row_index // PAIR_DEV * DATE_DEV
    local_offset = jax.random.randint(subkeys[0], (PAIRS,), 0, DATE_DEV, dtype=jnp.int32)
    local_offset = jnp.where(row_index % PAIR_DEV == 0, 0, local_offset)
    reference_date = jnp.minimum(first_date + local_offset, DATES - 2)
    date_lag = jax.random.randint(subkeys[1], (PAIRS,), 1, DATE_DEV + 1, dtype=jnp.int32)
    secondary = jnp.minimum(reference_date + date_lag, DATES - 1)
    return jnp.stack([reference_date, secondary], axis=1).astype(jnp.int32)


def setup_inputs(seed: int = 0, part: int = 0) -> dict:
    arg_keys = jax.random.split(jax.random.key(seed), 4)
    part_splits = jax.random.split(jax.random.fold_in(arg_keys[3], part), 4)
    slc_tiles = draw_slc_tiles(jax.random.fold_in(jax.random.fold_in(arg_keys[3], part), 71), part)
    look_weight = jnp.clip(jnp.exp(jax.random.uniform(part_splits[1], (ROWS, COLS), jnp.float32, math.log(0.05), math.log(1.0))), 0.05, 1.0)
    pair_list = draw_pair_list(jax.random.fold_in(arg_keys[3], 71), part)
    return dict(slc_tiles=slc_tiles, look_weight=look_weight, pair_list=pair_list)


def box_sum(values, col_count):
    rim_width = LOOK // 2
    row_count = values.shape[-2]
    padded = jnp.pad(values, [(0, 0)] * (values.ndim - 2) + [(rim_width, rim_width), (0, 0)])
    running = padded[..., 0:row_count, :]
    for offset in range(1, LOOK):
        running = running + padded[..., offset:offset + row_count, :]
    summed = running[..., 0:col_count]
    for offset in range(1, LOOK):
        summed = summed + running[..., offset:offset + col_count]
    return summed

def observe(first_tile, second_tile, weight, col_count):
    first_re = first_tile[..., 0, :, :].astype(jnp.float32)
    first_im = first_tile[..., 1, :, :].astype(jnp.float32)
    second_re = second_tile[..., 0, :, :].astype(jnp.float32)
    second_im = second_tile[..., 1, :, :].astype(jnp.float32)
    cross_re = weight * (first_re * second_re + first_im * second_im)
    cross_im = weight * (first_im * second_re - first_re * second_im)
    power_first = weight * (first_re * first_re + first_im * first_im)
    power_second = weight * (second_re * second_re + second_im * second_im)
    stacked = jnp.stack([cross_re, cross_im, power_first, power_second], axis=0)
    looked = box_sum(stacked, col_count)
    return (looked[1] * lax.rsqrt(looked[2] * looked[3] + 1e-06)).astype(jnp.bfloat16)

def solve_normal(normal_matrix, projected):
    factor = jnp.linalg.cholesky(normal_matrix)
    return jax.scipy.linalg.cho_solve((factor, True), projected)

def reference(slc_tiles, look_weight, pair_list):
    rim_width = LOOK // 2
    tiles_pad = jnp.pad(slc_tiles, ((0, 0), (0, 0), (0, 0), (rim_width, rim_width)))
    weight_pad = jnp.pad(look_weight, ((0, 0), (rim_width, rim_width)))

    def one_pair(pair_row):
        return observe(tiles_pad[pair_row[0]], tiles_pad[pair_row[1]], weight_pad, COLS)
    observed = lax.map(one_pair, pair_list)
    date_ids = jnp.arange(DATES, dtype=jnp.int32)
    incidence = ((date_ids[:, None] == pair_list[None, :, 0]).astype(jnp.float32) - (date_ids[:, None] == pair_list[None, :, 1]).astype(jnp.float32)).astype(jnp.bfloat16)
    normal_matrix = jnp.dot(incidence.astype(jnp.float32), incidence.T.astype(jnp.float32), preferred_element_type=jnp.float32) + jnp.eye(DATES, dtype=jnp.float32)
    projected = jnp.dot(incidence.astype(jnp.float32), observed.reshape(PAIRS, ROWS * COLS).astype(jnp.float32), preferred_element_type=jnp.float32)
    series = solve_normal(normal_matrix, projected).reshape(DATES, ROWS, COLS)
    columns = (2.0 * jnp.arange(COLS, dtype=jnp.int32).astype(jnp.float32) + 1.0) / COLS - 1.0
    square_sum = jnp.sum(columns * columns)
    date_mean = lax.optimization_barrier(jnp.sum(series, axis=(1, 2))) / (ROWS * COLS)
    date_slope = lax.optimization_barrier(jnp.sum(series * columns, axis=(1, 2))) / (ROWS * square_sum)
    return series - date_mean[:, None, None] - date_slope[:, None, None] * columns
```

```python
import functools

import jax
import jax.numpy as jnp
from jax import lax
from jax.experimental import pallas as pl
from jax.experimental.pallas import tpu as pltpu
from jax.sharding import PartitionSpec as P

LOOK = 9
RIM = LOOK // 2
LAGS = 4
SUB = 8
LANES = 128
EDGE = 2 * RIM
HALF = LANES // EDGE

F32 = jnp.float32
BF16 = jnp.bfloat16


def iota2(shape, dim):
    return lax.broadcasted_iota(jnp.int32, shape, dim)


def split2(value):
    high = value.astype(BF16)
    low = (value - high.astype(F32)).astype(BF16)
    return high, low


def window_rows(rows, count):
    def add(a, b):
        return b if a is None else (a if b is None else a + b)

    def at(series, i):
        return series.get(i)

    base = {i: rows[i] for i in range(count)}
    two = {i: add(at(base, i), at(base, i + 1)) for i in range(-RIM, count)}
    four = {i: add(at(two, i), at(two, i + 2)) for i in range(-RIM, count)}
    eight = {i: add(at(four, i), at(four, i + 4)) for i in range(-RIM, count)}
    return [add(at(eight, r - RIM), at(base, r + RIM)) for r in range(count)]


def column_band():
    source = lax.rem(iota2((2 * LANES, LANES), 0), LANES)
    return (jnp.abs(source - iota2((2 * LANES, LANES), 1)) <= RIM).astype(BF16)


def edge_matrix(row_count):
    size = row_count * EDGE
    source, target = iota2((size, size), 0), iota2((size, size), 1)
    near = jnp.abs(source // EDGE - target // EDGE) <= RIM
    e, t = source % EDGE, target % EDGE
    left = (e < RIM) & (t >= RIM) & (e >= t - RIM)
    right = (e >= RIM) & (t < RIM) & (t >= e - RIM)
    return (near & (left | right)).astype(BF16)


def observe_kernel(
    row_count, unit_count,
    pair_ref, next_ref, weight_ref, edge_weight_ref, band_ref, edge_ref, solve_ref, coord_ref,
    series_ref, sums_ref,
    re_s, im_s, pw_s, hre_s, him_s, obs_s,
):
    unit = pl.program_id(0)
    slots = 2 * SUB
    halves = row_count // HALF
    date_dev = next_ref.shape[1] // (2 * row_count)
    hbase = 2 * date_dev * row_count

    def place(block, at):
        for d in range(date_dev):
            for c, dst in ((0, re_s), (1, im_s)):
                start = (d * 2 + c) * row_count
                values = block[start : start + row_count, :].astype(F32)
                for g in range(row_count // SUB):
                    dst[pl.ds(g * SUB * slots + at + d, SUB, stride=slots), :] = values[g * SUB : (g + 1) * SUB]
        edge = block[hbase : hbase + 2 * halves * date_dev, :].astype(F32)
        for c, dst in ((0, hre_s), (1, him_s)):
            for h in range(halves):
                start = (c * halves + h) * date_dev
                dst[pl.ds(h * slots + at, date_dev), :] = edge[start : start + date_dev]

    per_unit = pair_ref.shape[0]
    for s in range(per_unit):
        place(pair_ref[s], s * date_dev)
    place(next_ref[0], per_unit * date_dev)

    def products(re, im, weights, count):
        images = [[] for _ in range(2 + LAGS)]
        for r in range(count):
            w = weights[pl.ds(r, 1), :]
            a_re, a_im = re[pl.ds(r * slots, SUB), :], im[pl.ds(r * slots, SUB), :]
            n_re, n_im = re[pl.ds(r * slots + SUB, SUB), :], im[pl.ds(r * slots + SUB, SUB), :]
            images[0].append(w * (a_re * a_re + a_im * a_im))
            images[1].append(w * (n_re * n_re + n_im * n_im))
        for lag in range(1, LAGS + 1):
            for r in range(count):
                w = weights[pl.ds(r, 1), :]
                a_re, a_im = re[pl.ds(r * slots, SUB), :], im[pl.ds(r * slots, SUB), :]
                b_re, b_im = re[pl.ds(r * slots + lag, SUB), :], im[pl.ds(r * slots + lag, SUB), :]
                images[1 + lag].append(w * (a_im * b_re - a_re * b_im))
        return images

    halo = products(hre_s, him_s, edge_weight_ref, halves)
    halo = jnp.concatenate([jnp.concatenate(image, axis=1) for image in halo], axis=0)
    high, low = split2(halo)
    edge = edge_ref[...]
    edges = jnp.dot(high, edge, preferred_element_type=F32) + jnp.dot(low, edge, preferred_element_type=F32)

    lane = iota2((SUB, LANES), 1)
    at_edge = (lane >= LANES - RIM) | (lane < RIM)
    images = products(re_s, im_s, weight_ref, row_count)
    band = band_ref[...]

    def look(which):
        rows = jnp.concatenate(window_rows(images[which], row_count), axis=0)
        summed = jnp.dot(jnp.concatenate(split2(rows), axis=1), band, preferred_element_type=F32)
        out = []
        for r in range(row_count):
            tile = edges[which * SUB : (which + 1) * SUB, (r // HALF) * LANES : (r // HALF + 1) * LANES]
            shift = (LANES - RIM - EDGE * (r % HALF)) % LANES
            rolled = pltpu.roll(tile, shift, 1)
            out.append(summed[r * SUB : (r + 1) * SUB] + jnp.where(at_edge, rolled, 0.0))
        return out

    for part in range(2):
        for r, value in enumerate(look(part)):
            pw_s[pl.ds(r * slots + part * SUB, SUB), :] = value

    def observed(lag):
        out = []
        for r, value in enumerate(look(1 + lag)):
            p = pw_s[pl.ds(r * slots, SUB), :]
            q = pw_s[pl.ds(r * slots + lag, SUB), :]
            out.append(value * lax.rsqrt(p * q + 1e-06))
        return out

    combos = unit_count * SUB * LAGS
    for lag in range(1, LAGS + 1, 2):
        first, second = observed(lag), observed(lag + 1)
        for r in range(row_count):
            at = pl.multiple_of(r * combos + unit * (SUB * LAGS) + (lag - 1) * SUB, 2 * SUB)
            obs_s[pl.ds(at, 2 * SUB), :] = jnp.concatenate([first[r], second[r]], axis=0).astype(BF16)

    @pl.when(unit == unit_count - 1)
    def _():
        solve = solve_ref[...]
        date_total = solve.shape[0] // 2
        mean = jnp.zeros((date_total, LANES), F32)
        for r in range(row_count):
            both = jnp.dot(solve, obs_s[pl.ds(r * combos, combos), :], preferred_element_type=F32)
            series = both[:date_total] + both[date_total:]
            series_ref[:, r, :] = series
            mean = mean + series
        slope = mean * coord_ref[...]
        sums_ref[:, pl.ds(0, 1)] = jnp.sum(mean, axis=1, keepdims=True)
        sums_ref[:, pl.ds(1, 1)] = jnp.sum(slope, axis=1, keepdims=True)


def observe_all(blocks, weight, edge_weight, solve, coord, row_count, date_dev):
    per_unit = SUB // date_dev
    unit_count = blocks.shape[0] // per_unit
    date_total = unit_count * SUB
    combos = date_total * LAGS
    block_rows = blocks.shape[1]
    halves = row_count // HALF
    slots = 2 * SUB
    whole = lambda a: pl.BlockSpec(a.shape, lambda u: (0,) * a.ndim)
    band, edge = column_band(), edge_matrix(row_count)
    sources = blocks.shape[0]
    return pl.pallas_call(
        functools.partial(observe_kernel, row_count, unit_count),
        grid=(unit_count,),
        out_shape=(
            jax.ShapeDtypeStruct((date_total, row_count, LANES), F32),
            jax.ShapeDtypeStruct((date_total, 2), F32),
        ),
        in_specs=[
            pl.BlockSpec((per_unit, block_rows, LANES), lambda u: (u, 0, 0)),
            pl.BlockSpec((1, block_rows, LANES), lambda u: (lax.rem(u * per_unit + per_unit, sources), 0, 0)),
            whole(weight), whole(edge_weight), whole(band), whole(edge), whole(solve), whole(coord),
        ],
        out_specs=(
            pl.BlockSpec((date_total, row_count, LANES), lambda u: (0, 0, 0)),
            pl.BlockSpec((date_total, 2), lambda u: (0, 0)),
        ),
        scratch_shapes=[
            pltpu.VMEM((row_count * slots, LANES), F32),
            pltpu.VMEM((row_count * slots, LANES), F32),
            pltpu.VMEM((row_count * slots, LANES), F32),
            pltpu.VMEM((halves * slots, LANES), F32),
            pltpu.VMEM((halves * slots, LANES), F32),
            pltpu.VMEM((row_count * combos, LANES), BF16),
        ],
        compiler_params=pltpu.CompilerParams(dimension_semantics=("arbitrary",)),
        name="observe",
    )(blocks, blocks, weight, edge_weight, band, edge, solve, coord)


def solve_matrix(pair_list, date_total):
    first, lag = pair_list[:, 0], pair_list[:, 1] - pair_list[:, 0]
    dates = lax.iota(jnp.int32, date_total)
    at_first = (dates[:, None] == first[None, :]).astype(F32)
    at_second = (dates[:, None] == pair_list[None, :, 1]).astype(F32)
    incidence = (at_first - at_second).astype(BF16)
    normal_matrix = jnp.dot(incidence, incidence.T, preferred_element_type=F32) + jnp.eye(date_total, dtype=F32)
    factor = jnp.linalg.cholesky(normal_matrix)
    lags = lax.iota(jnp.int32, LAGS) + 1
    at_lag = (lags[:, None] == lag[None, :]).astype(BF16)
    count = jnp.dot(at_lag, at_first.astype(BF16).T, preferred_element_type=F32)
    second = dates[None, :] + lags[:, None]
    ends = (dates[:, None, None] == dates[None, None, :]).astype(F32) - (
        dates[:, None, None] == second[None]
    ).astype(F32)
    columns = ends * count[None]
    units = date_total // SUB
    columns = columns.reshape(date_total, LAGS, units, SUB).transpose(0, 2, 1, 3).reshape(date_total, LAGS * date_total)
    solved = jax.scipy.linalg.cho_solve((factor, True), columns)
    return jnp.concatenate(split2(solved), axis=0)


def body(slc_tiles, look_weight, pair_list):
    devices = lax.axis_size("gx")
    position = lax.axis_index("gx")
    date_dev, _, row_count, col_total = slc_tiles.shape
    strip = col_total // devices
    date_total = date_dev * devices
    halves = row_count // HALF

    main = slc_tiles.reshape(date_dev, 2, row_count, devices, strip).transpose(3, 0, 1, 2, 4)
    main = main.reshape(devices, date_dev * 2 * row_count, strip)
    padded = jnp.pad(slc_tiles, ((0, 0), (0, 0), (0, 0), (RIM, RIM)))
    left = padded[..., :col_total].reshape(date_dev, 2, row_count, devices, strip)[..., :RIM]
    right = padded[..., EDGE:].reshape(date_dev, 2, row_count, devices, strip)[..., strip - RIM :]
    halo = jnp.concatenate([left, right], axis=-1).reshape(date_dev, 2, halves, HALF, devices, EDGE)
    halo = halo.transpose(4, 1, 2, 0, 3, 5).reshape(devices, 2 * halves * date_dev, LANES)
    blocks = lax.all_to_all(jnp.concatenate([main, halo], axis=1), "gx", 0, 0, tiled=True)

    weight = lax.dynamic_slice_in_dim(look_weight, position * strip, strip, 1)
    weight_pad = jnp.pad(look_weight, ((0, 0), (RIM, RIM)))
    edge_weight = jnp.concatenate(
        [
            lax.dynamic_slice_in_dim(weight_pad, position * strip, RIM, 1),
            lax.dynamic_slice_in_dim(weight_pad, position * strip + strip + RIM, RIM, 1),
        ],
        axis=1,
    ).reshape(halves, LANES)
    solve = solve_matrix(pair_list, date_total)
    all_cols = (2.0 * lax.iota(jnp.int32, col_total).astype(F32) + 1.0) / col_total - 1.0
    square_sum = jnp.sum(all_cols * all_cols)
    column_ids = position * strip + lax.iota(jnp.int32, strip)
    columns = (2.0 * column_ids.astype(F32) + 1.0) / col_total - 1.0

    series, sums = observe_all(blocks, weight, edge_weight, solve, columns[None], row_count, date_dev)
    step = 1
    while step < devices:
        sums = sums + lax.ppermute(sums, "gx", [(s, s ^ step) for s in range(devices)])
        step *= 2
    date_mean = sums[:, 0] / (row_count * col_total)
    date_slope = sums[:, 1] / (row_count * square_sum)
    return series - date_mean[:, None, None] - date_slope[:, None, None] * columns


def solution(mesh):
    return jax.shard_map(
        body,
        mesh=mesh,
        in_specs=(P("gx", None, "band", None), P("band", None), P()),
        out_specs=P(None, "band", "gx"),
        check_vma=False,
    )
```

```python
import functools

import jax
import jax.numpy as jnp
from jax import lax
from jax.experimental import pallas as pl
from jax.experimental.pallas import tpu as pltpu
from jax.sharding import PartitionSpec as P

LOOK = 9
RIM = LOOK // 2
LAGS = 4
SUB = 8
LANES = 128
EDGE = 2 * RIM
HALF = LANES // EDGE

F32 = jnp.float32
BF16 = jnp.bfloat16


def iota2(shape, dim):
    return lax.broadcasted_iota(jnp.int32, shape, dim)


def split2(value):
    high = value.astype(BF16)
    low = (value - high.astype(F32)).astype(BF16)
    return high, low


def window_rows(rows, count):
    def add(a, b):
        return b if a is None else (a if b is None else a + b)

    def at(series, i):
        return series.get(i)

    base = {i: rows[i] for i in range(count)}
    two = {i: add(at(base, i), at(base, i + 1)) for i in range(-RIM, count)}
    four = {i: add(at(two, i), at(two, i + 2)) for i in range(-RIM, count)}
    eight = {i: add(at(four, i), at(four, i + 4)) for i in range(-RIM, count)}
    return [add(at(eight, r - RIM), at(base, r + RIM)) for r in range(count)]


def column_band():
    source = lax.rem(iota2((2 * LANES, LANES), 0), LANES)
    return (jnp.abs(source - iota2((2 * LANES, LANES), 1)) <= RIM).astype(BF16)


def edge_matrix(row_count):
    size = row_count * EDGE
    source, target = iota2((size, size), 0), iota2((size, size), 1)
    near = jnp.abs(source // EDGE - target // EDGE) <= RIM
    e, t = source % EDGE, target % EDGE
    left = (e < RIM) & (t >= RIM) & (e >= t - RIM)
    right = (e >= RIM) & (t < RIM) & (t >= e - RIM)
    return (near & (left | right)).astype(BF16)


def observe_kernel(
    row_count, unit_count,
    pair_ref, next_ref, weight_ref, edge_weight_ref, band_ref, edge_ref, solve_ref, coord_ref,
    series_ref, sums_ref,
    re_s, im_s, pw_s, hre_s, him_s, obs_s,
):
    unit = pl.program_id(0)
    slots = 2 * SUB
    halves = row_count // HALF
    date_dev = next_ref.shape[1] // (2 * row_count)
    hbase = 2 * date_dev * row_count

    def place(block, at):
        for d in range(date_dev):
            for c, dst in ((0, re_s), (1, im_s)):
                start = (d * 2 + c) * row_count
                values = block[start : start + row_count, :].astype(F32)
                for g in range(row_count // SUB):
                    dst[pl.ds(g * SUB * slots + at + d, SUB, stride=slots), :] = values[g * SUB : (g + 1) * SUB]
        edge = block[hbase : hbase + 2 * halves * date_dev, :].astype(F32)
        for c, dst in ((0, hre_s), (1, him_s)):
            for h in range(halves):
                start = (c * halves + h) * date_dev
                dst[pl.ds(h * slots + at, date_dev), :] = edge[start : start + date_dev]

    per_unit = pair_ref.shape[0]
    for s in range(per_unit):
        place(pair_ref[s], s * date_dev)
    place(next_ref[0], per_unit * date_dev)

    def products(re, im, weights, count):
        images = [[] for _ in range(2 + LAGS)]
        for r in range(count):
            w = weights[pl.ds(r, 1), :]
            a_re, a_im = re[pl.ds(r * slots, SUB), :], im[pl.ds(r * slots, SUB), :]
            n_re, n_im = re[pl.ds(r * slots + SUB, SUB), :], im[pl.ds(r * slots + SUB, SUB), :]
            images[0].append(w * (a_re * a_re + a_im * a_im))
            images[1].append(w * (n_re * n_re + n_im * n_im))
        for lag in range(1, LAGS + 1):
            for r in range(count):
                w = weights[pl.ds(r, 1), :]
                a_re, a_im = re[pl.ds(r * slots, SUB), :], im[pl.ds(r * slots, SUB), :]
                b_re, b_im = re[pl.ds(r * slots + lag, SUB), :], im[pl.ds(r * slots + lag, SUB), :]
                images[1 + lag].append(w * (a_im * b_re - a_re * b_im))
        return images

    halo = products(hre_s, him_s, edge_weight_ref, halves)
    halo = jnp.concatenate([jnp.concatenate(image, axis=1) for image in halo], axis=0)
    high, low = split2(halo)
    edge = edge_ref[...]
    edges = jnp.dot(high, edge, preferred_element_type=F32) + jnp.dot(low, edge, preferred_element_type=F32)

    lane = iota2((SUB, LANES), 1)
    at_edge = (lane >= LANES - RIM) | (lane < RIM)
    images = products(re_s, im_s, weight_ref, row_count)
    band = band_ref[...]

    def look(which):
        rows = jnp.concatenate(window_rows(images[which], row_count), axis=0)
        summed = jnp.dot(jnp.concatenate(split2(rows), axis=1), band, preferred_element_type=F32)
        out = []
        for r in range(row_count):
            tile = edges[which * SUB : (which + 1) * SUB, (r // HALF) * LANES : (r // HALF + 1) * LANES]
            shift = (LANES - RIM - EDGE * (r % HALF)) % LANES
            rolled = pltpu.roll(tile, shift, 1)
            out.append(summed[r * SUB : (r + 1) * SUB] + jnp.where(at_edge, rolled, 0.0))
        return out

    for part in range(2):
        for r, value in enumerate(look(part)):
            pw_s[pl.ds(r * slots + part * SUB, SUB), :] = value

    def observed(lag):
        out = []
        for r, value in enumerate(look(1 + lag)):
            p = pw_s[pl.ds(r * slots, SUB), :]
            q = pw_s[pl.ds(r * slots + lag, SUB), :]
            out.append(value * lax.rsqrt(p * q + 1e-06))
        return out

    combos = unit_count * SUB * LAGS
    for lag in range(1, LAGS + 1, 2):
        first, second = observed(lag), observed(lag + 1)
        for r in range(row_count):
            at = pl.multiple_of(r * combos + unit * (SUB * LAGS) + (lag - 1) * SUB, 2 * SUB)
            obs_s[pl.ds(at, 2 * SUB), :] = jnp.concatenate([first[r], second[r]], axis=0).astype(BF16)

    @pl.when(unit == unit_count - 1)
    def _():
        solve = solve_ref[...]
        date_total = solve.shape[0] // 2
        mean = jnp.zeros((date_total, LANES), F32)
        for r in range(row_count):
            both = jnp.dot(solve, obs_s[pl.ds(r * combos, combos), :], preferred_element_type=F32)
            series = both[:date_total] + both[date_total:]
            series_ref[:, r, :] = series
            mean = mean + series
        eye = iota2((date_total, date_total), 0) == iota2((date_total, date_total), 1)
        for i, part in enumerate((mean, mean * coord_ref[...])):
            column = jnp.sum(part, axis=1, keepdims=True)
            sums_ref[pl.ds(i, 1), :] = jnp.sum(jnp.where(eye, column, 0.0), axis=0, keepdims=True)


def observe_all(blocks, weight, edge_weight, solve, coord, row_count, date_dev):
    per_unit = SUB // date_dev
    unit_count = blocks.shape[0] // per_unit
    date_total = unit_count * SUB
    combos = date_total * LAGS
    block_rows = blocks.shape[1]
    halves = row_count // HALF
    slots = 2 * SUB
    whole = lambda a: pl.BlockSpec(a.shape, lambda u: (0,) * a.ndim)
    band, edge = column_band(), edge_matrix(row_count)
    sources = blocks.shape[0]
    return pl.pallas_call(
        functools.partial(observe_kernel, row_count, unit_count),
        grid=(unit_count,),
        out_shape=(
            jax.ShapeDtypeStruct((date_total, row_count, LANES), F32),
            jax.ShapeDtypeStruct((2, date_total), F32),
        ),
        in_specs=[
            pl.BlockSpec((per_unit, block_rows, LANES), lambda u: (u, 0, 0)),
            pl.BlockSpec((1, block_rows, LANES), lambda u: (lax.rem(u * per_unit + per_unit, sources), 0, 0)),
            whole(weight), whole(edge_weight), whole(band), whole(edge), whole(solve), whole(coord),
        ],
        out_specs=(
            pl.BlockSpec((date_total, row_count, LANES), lambda u: (0, 0, 0)),
            pl.BlockSpec((2, date_total), lambda u: (0, 0)),
        ),
        scratch_shapes=[
            pltpu.VMEM((row_count * slots, LANES), F32),
            pltpu.VMEM((row_count * slots, LANES), F32),
            pltpu.VMEM((row_count * slots, LANES), F32),
            pltpu.VMEM((halves * slots, LANES), F32),
            pltpu.VMEM((halves * slots, LANES), F32),
            pltpu.VMEM((row_count * combos, LANES), BF16),
        ],
        compiler_params=pltpu.CompilerParams(dimension_semantics=("arbitrary",)),
        name="observe",
    )(blocks, blocks, weight, edge_weight, band, edge, solve, coord)


def pack_kernel(date_dev, row_count, tiles_ref, out_ref):
    strips = out_ref.shape[0]
    size = tiles_ref.shape[0]
    halves = row_count // HALF
    source, lane = iota2((2 * LANES, LANES), 0), iota2((2 * LANES, LANES), 1) % EDGE
    spread = (lane == jnp.where(source < LANES, source - (LANES - RIM), source - LANES + RIM)) & (
        (source >= LANES) == (lane >= RIM)
    )
    spread = spread.astype(BF16)
    mask = iota2((size, LANES), 0) % HALF == iota2((size, LANES), 1) // EDGE
    out_rows = 2 * halves * date_dev
    target, row = iota2((out_rows, size), 0), iota2((out_rows, size), 1)
    same = (
        (target % date_dev == row // (2 * row_count))
        & (target // (halves * date_dev) == row // row_count % 2)
        & (target // date_dev % halves == row // HALF % halves)
    ).astype(BF16)
    nothing = jnp.zeros((size, LANES), BF16)
    for j in range(strips):
        out_ref[j, pl.ds(0, size), :] = tiles_ref[:, j * LANES : (j + 1) * LANES]
        before = tiles_ref[:, (j - 1) * LANES : j * LANES] if j else nothing
        after = tiles_ref[:, (j + 1) * LANES : (j + 2) * LANES] if j + 1 < strips else nothing
        copies = jnp.dot(jnp.concatenate([before, after], axis=1), spread, preferred_element_type=F32)
        copies = jnp.where(mask, copies, 0.0).astype(BF16)
        edge = jnp.dot(same, copies, preferred_element_type=F32)
        out_ref[j, pl.ds(size, out_rows), :] = edge.astype(BF16)


def pack(tiles, devices):
    date_dev, _, row_count, col_total = tiles.shape
    size = date_dev * 2 * row_count
    block_rows = size + 2 * (row_count // HALF) * date_dev
    return pl.pallas_call(
        functools.partial(pack_kernel, date_dev, row_count),
        out_shape=jax.ShapeDtypeStruct((devices, block_rows, LANES), BF16),
        in_specs=[pl.BlockSpec(memory_space=pltpu.VMEM)],
        out_specs=pl.BlockSpec(memory_space=pltpu.VMEM),
        name="pack",
    )(tiles.reshape(size, col_total))


def remove_kernel(pixels, series_ref, sums_ref, coord_ref, out_ref):
    dates = series_ref.shape[0]
    eye = iota2((dates, dates), 0) == iota2((dates, dates), 1)
    mean = jnp.sum(jnp.where(eye, sums_ref[pl.ds(0, 1), :], 0.0), axis=1, keepdims=True) / pixels
    slope = jnp.sum(jnp.where(eye, sums_ref[pl.ds(1, 1), :], 0.0), axis=1, keepdims=True)
    coord = coord_ref[pl.ds(0, 1), :]
    slope = slope / coord_ref[pl.ds(1, 1), pl.ds(0, 1)]
    trend = mean + slope * coord
    for r in range(series_ref.shape[1]):
        out_ref[:, r, :] = series_ref[:, r, :] - trend


def solve_matrix(pair_list, date_total):
    first, lag = pair_list[:, 0], pair_list[:, 1] - pair_list[:, 0]
    dates = lax.iota(jnp.int32, date_total)
    at_first = (dates[:, None] == first[None, :]).astype(F32)
    at_second = (dates[:, None] == pair_list[None, :, 1]).astype(F32)
    incidence = (at_first - at_second).astype(BF16)
    normal_matrix = jnp.dot(incidence, incidence.T, preferred_element_type=F32) + jnp.eye(date_total, dtype=F32)
    factor = jnp.linalg.cholesky(normal_matrix)
    lags = lax.iota(jnp.int32, LAGS) + 1
    at_lag = (lags[:, None] == lag[None, :]).astype(BF16)
    count = jnp.dot(at_lag, at_first.astype(BF16).T, preferred_element_type=F32)
    second = dates[None, :] + lags[:, None]
    ends = (dates[:, None, None] == dates[None, None, :]).astype(F32) - (
        dates[:, None, None] == second[None]
    ).astype(F32)
    columns = ends * count[None]
    units = date_total // SUB
    columns = columns.reshape(date_total, LAGS, units, SUB).transpose(0, 2, 1, 3).reshape(date_total, LAGS * date_total)
    solved = jax.scipy.linalg.cho_solve((factor, True), columns)
    return jnp.concatenate(split2(solved), axis=0)


def body(slc_tiles, look_weight, pair_list):
    devices = lax.axis_size("gx")
    position = lax.axis_index("gx")
    date_dev, _, row_count, col_total = slc_tiles.shape
    strip = col_total // devices
    date_total = date_dev * devices
    halves = row_count // HALF

    blocks = lax.all_to_all(pack(slc_tiles, devices), "gx", 0, 0, tiled=True)

    weight = lax.dynamic_slice_in_dim(look_weight, position * strip, strip, 1)
    weight_pad = jnp.pad(look_weight, ((0, 0), (RIM, RIM)))
    edge_weight = jnp.concatenate(
        [
            lax.dynamic_slice_in_dim(weight_pad, position * strip, RIM, 1),
            lax.dynamic_slice_in_dim(weight_pad, position * strip + strip + RIM, RIM, 1),
        ],
        axis=1,
    ).reshape(halves, LANES)
    solve = solve_matrix(pair_list, date_total)
    all_cols = (2.0 * lax.iota(jnp.int32, col_total).astype(F32) + 1.0) / col_total - 1.0
    square_sum = jnp.sum(all_cols * all_cols)
    column_ids = position * strip + lax.iota(jnp.int32, strip)
    columns = (2.0 * column_ids.astype(F32) + 1.0) / col_total - 1.0

    series, sums = observe_all(blocks, weight, edge_weight, solve, columns[None], row_count, date_dev)
    step = 1
    while step < devices:
        sums = sums + lax.ppermute(sums, "gx", [(s, s ^ step) for s in range(devices)])
        step *= 2
    trend_coord = jnp.stack([columns, jnp.broadcast_to(row_count * square_sum, (strip,))])
    rows = SUB
    return pl.pallas_call(
        functools.partial(remove_kernel, row_count * col_total),
        grid=(row_count // rows,),
        out_shape=jax.ShapeDtypeStruct(series.shape, F32),
        in_specs=[
            pl.BlockSpec((date_total, rows, strip), lambda i: (0, i, 0)),
            pl.BlockSpec(sums.shape, lambda i: (0, 0)),
            pl.BlockSpec(trend_coord.shape, lambda i: (0, 0)),
        ],
        out_specs=pl.BlockSpec((date_total, rows, strip), lambda i: (0, i, 0)),
        name="remove",
    )(series, sums, trend_coord)


def solution(mesh):
    return jax.shard_map(
        body,
        mesh=mesh,
        in_specs=(P("gx", None, "band", None), P("band", None), P()),
        out_specs=P(None, "band", "gx"),
        check_vma=False,
    )
```

```python
import functools

import jax
import jax.numpy as jnp
from jax import lax
from jax.experimental import pallas as pl
from jax.experimental.pallas import tpu as pltpu
from jax.sharding import PartitionSpec as P

LOOK = 9
RIM = LOOK // 2
LAGS = 4
SUB = 8
LANES = 128
EDGE = 2 * RIM
HALF = LANES // EDGE

F32 = jnp.float32
BF16 = jnp.bfloat16


def iota2(shape, dim):
    return lax.broadcasted_iota(jnp.int32, shape, dim)


def split2(value):
    high = value.astype(BF16)
    low = (value - high.astype(F32)).astype(BF16)
    return high, low


def window_rows(rows, count):
    def add(a, b):
        return b if a is None else (a if b is None else a + b)

    def at(series, i):
        return series.get(i)

    base = {i: rows[i] for i in range(count)}
    two = {i: add(at(base, i), at(base, i + 1)) for i in range(-RIM, count)}
    four = {i: add(at(two, i), at(two, i + 2)) for i in range(-RIM, count)}
    eight = {i: add(at(four, i), at(four, i + 4)) for i in range(-RIM, count)}
    return [add(at(eight, r - RIM), at(base, r + RIM)) for r in range(count)]


def column_band():
    source = lax.rem(iota2((2 * LANES, LANES), 0), LANES)
    return (jnp.abs(source - iota2((2 * LANES, LANES), 1)) <= RIM).astype(BF16)


def edge_matrix(row_count):
    size = row_count * EDGE
    source, target = iota2((size, size), 0), iota2((size, size), 1)
    near = jnp.abs(source // EDGE - target // EDGE) <= RIM
    e, t = source % EDGE, target % EDGE
    left = (e < RIM) & (t >= RIM) & (e >= t - RIM)
    right = (e >= RIM) & (t < RIM) & (t >= e - RIM)
    return (near & (left | right)).astype(BF16)


def observe_kernel(
    row_count, unit_count,
    group_ref, weight_ref, edge_weight_ref, band_ref, edge_ref, solve_ref, coord_ref,
    series_ref, sums_ref,
    re_s, im_s, wre_s, wim_s, pw_s, hre_s, him_s, hwre_s, hwim_s, obs_s,
):
    group = pl.program_id(0)
    slots = (unit_count + 1) * SUB
    halves = row_count // HALF
    per_unit, block_rows, _ = group_ref.shape
    date_dev = SUB // per_unit
    hbase = 2 * date_dev * row_count
    new = pl.multiple_of(group * SUB, SUB)

    for s in range(per_unit):
        for d in range(date_dev):
            for c, dst in ((0, re_s), (1, im_s)):
                start = (d * 2 + c) * row_count
                values = group_ref[s, pl.ds(start, row_count), :].astype(F32)
                for g in range(row_count // SUB):
                    at = pl.ds(g * SUB * slots + new + s * date_dev + d, SUB, stride=slots)
                    dst[at, :] = values[g * SUB : (g + 1) * SUB]
        edge = group_ref[s, pl.ds(hbase, 2 * halves * date_dev), :].astype(F32)
        for c, dst in ((0, hre_s), (1, him_s)):
            for h in range(halves):
                start = (c * halves + h) * date_dev
                dst[pl.ds(h * slots + new + s * date_dev, date_dev), :] = edge[start : start + date_dev]

    lane = iota2((SUB, LANES), 1)
    at_edge = (lane >= LANES - RIM) | (lane < RIM)

    def power(re, im, wre, wim, weights, count):
        out = []
        for r in range(count):
            at = pl.ds(r * slots + new, SUB)
            w = weights[pl.ds(r, 1), :]
            a_re, a_im = re[at, :], im[at, :]
            w_re, w_im = w * a_re, w * a_im
            wre[at, :] = w_re
            wim[at, :] = w_im
            out.append(w_re * a_re + w_im * a_im)
        return out

    def cross(re, im, wre, wim, count, lag, old):
        out = []
        for r in range(count):
            at, ahead = pl.ds(r * slots + old, SUB), pl.ds(r * slots + old + lag, SUB)
            out.append(wim[at, :] * re[ahead, :] - wre[at, :] * im[ahead, :])
        return out

    def at_edges(images):
        halo = jnp.concatenate([jnp.concatenate(image, axis=1) for image in images], axis=0)
        summed = jnp.dot(jnp.concatenate(split2(halo), axis=0), edge_ref[...], preferred_element_type=F32)
        return summed[: halo.shape[0]] + summed[halo.shape[0] :]

    def look(image, edges):
        rows = jnp.concatenate(window_rows(image, row_count), axis=0)
        summed = jnp.dot(jnp.concatenate(split2(rows), axis=1), band_ref[...], preferred_element_type=F32)
        out = []
        for r in range(row_count):
            tile = edges[:, (r // HALF) * LANES : (r // HALF + 1) * LANES]
            rolled = pltpu.roll(tile, (LANES - RIM - EDGE * (r % HALF)) % LANES, 1)
            out.append(summed[r * SUB : (r + 1) * SUB] + jnp.where(at_edge, rolled, 0.0))
        return out

    edges = at_edges([power(hre_s, him_s, hwre_s, hwim_s, edge_weight_ref, halves)])
    for r, value in enumerate(look(power(re_s, im_s, wre_s, wim_s, weight_ref, row_count), edges)):
        pw_s[pl.ds(r * slots + new, SUB), :] = value

    combos = unit_count * SUB * LAGS

    @pl.when(group > 0)
    def _():
        unit = group - 1
        old = pl.multiple_of(unit * SUB, SUB)
        lags = range(1, LAGS + 1)
        edges = at_edges([cross(hre_s, him_s, hwre_s, hwim_s, halves, lag, old) for lag in lags])

        def observed(lag):
            image = cross(re_s, im_s, wre_s, wim_s, row_count, lag, old)
            out = []
            for r, value in enumerate(look(image, edges[(lag - 1) * SUB : lag * SUB])):
                p = pw_s[pl.ds(r * slots + old, SUB), :]
                q = pw_s[pl.ds(r * slots + old + lag, SUB), :]
                out.append(value * lax.rsqrt(p * q + 1e-06))
            return out

        for lag in range(1, LAGS + 1, 2):
            first, second = observed(lag), observed(lag + 1)
            for r in range(row_count):
                at = pl.multiple_of(r * combos + unit * (SUB * LAGS) + (lag - 1) * SUB, 2 * SUB)
                obs_s[pl.ds(at, 2 * SUB), :] = jnp.concatenate([first[r], second[r]], axis=0).astype(BF16)

    @pl.when(group == unit_count)
    def _():
        solve = solve_ref[...]
        date_total = solve.shape[0] // 2
        mean = jnp.zeros((date_total, LANES), F32)
        for r in range(row_count):
            both = jnp.dot(solve, obs_s[pl.ds(r * combos, combos), :], preferred_element_type=F32)
            series = both[:date_total] + both[date_total:]
            for g in range(date_total // SUB):
                series_ref[pl.ds(g * SUB * row_count + r, SUB, stride=row_count), :] = series[g * SUB : (g + 1) * SUB]
            mean = mean + series
        eye = iota2((date_total, date_total), 0) == iota2((date_total, date_total), 1)
        for i, part in enumerate((mean, mean * coord_ref[...])):
            column = jnp.sum(part, axis=1, keepdims=True)
            sums_ref[pl.ds(i, 1), :] = jnp.sum(jnp.where(eye, column, 0.0), axis=0, keepdims=True)


def observe_all(blocks, weight, edge_weight, solve, coord, row_count, date_dev):
    per_unit = SUB // date_dev
    sources, block_rows, _ = blocks.shape
    unit_count = sources // per_unit
    date_total = unit_count * SUB
    combos = date_total * LAGS
    halves = row_count // HALF
    slots = (unit_count + 1) * SUB
    whole = lambda a: pl.BlockSpec(a.shape, lambda u: (0,) * a.ndim)
    band, edge = column_band(), edge_matrix(row_count)
    scratch = [pltpu.VMEM((row_count * slots, LANES), F32)] * 5
    scratch += [pltpu.VMEM((halves * slots, LANES), F32)] * 4
    scratch += [pltpu.VMEM((row_count * combos, LANES), BF16)]
    words = row_count * LANES * (5 * slots + combos // 2 + 2 * date_total) + date_total * LANES * combos // 64
    return pl.pallas_call(
        functools.partial(observe_kernel, row_count, unit_count),
        grid=(unit_count + 1,),
        out_shape=(
            jax.ShapeDtypeStruct((date_total * row_count, LANES), F32),
            jax.ShapeDtypeStruct((2, date_total), F32),
        ),
        in_specs=[
            pl.BlockSpec((per_unit, block_rows, LANES), lambda u: (lax.rem(u, unit_count), 0, 0)),
            whole(weight), whole(edge_weight), whole(band), whole(edge), whole(solve), whole(coord),
        ],
        out_specs=(
            pl.BlockSpec((date_total * row_count, LANES), lambda u: (0, 0)),
            pl.BlockSpec((2, date_total), lambda u: (0, 0)),
        ),
        scratch_shapes=scratch,
        compiler_params=pltpu.CompilerParams(
            dimension_semantics=("arbitrary",), vmem_limit_bytes=min(4 * words + 2**23, 2**26 - 2**17)
        ),
        name="observe",
    )(blocks, weight, edge_weight, band, edge, solve, coord)


def pack_kernel(date_dev, row_count, tiles_ref, out_ref, copies_s):
    strips = out_ref.shape[0]
    size = tiles_ref.shape[0]
    halves = row_count // HALF
    source, lane = iota2((2 * LANES, LANES), 0), iota2((2 * LANES, LANES), 1) % EDGE
    spread = (lane == jnp.where(source < LANES, source - (LANES - RIM), source - LANES + RIM)) & (
        (source >= LANES) == (lane >= RIM)
    )
    spread = spread.astype(BF16)
    mask = iota2((size, LANES), 0) % HALF == iota2((size, LANES), 1) // EDGE
    out_rows = 2 * halves * date_dev
    target, row = iota2((out_rows, size), 0), iota2((out_rows, size), 1)
    same = (
        (target % date_dev == row // (2 * row_count))
        & (target // (halves * date_dev) == row // row_count % 2)
        & (target // date_dev % halves == row // HALF % halves)
    ).astype(BF16)
    nothing = jnp.zeros((size, LANES), BF16)
    for j in range(strips):
        before = tiles_ref[:, (j - 1) * LANES : j * LANES] if j else nothing
        after = tiles_ref[:, (j + 1) * LANES : (j + 2) * LANES] if j + 1 < strips else nothing
        copies = jnp.dot(jnp.concatenate([before, after], axis=1), spread, preferred_element_type=F32)
        copies_s[:, j * LANES : (j + 1) * LANES] = jnp.where(mask, copies, 0.0).astype(BF16)
    for j in range(strips):
        out_ref[j, pl.ds(0, size), :] = tiles_ref[:, j * LANES : (j + 1) * LANES]
    edge = jnp.dot(same, copies_s[...], preferred_element_type=F32).astype(BF16)
    for j in range(strips):
        out_ref[j, pl.ds(size, out_rows), :] = edge[:, j * LANES : (j + 1) * LANES]


def pack(tiles, devices):
    date_dev, _, row_count, col_total = tiles.shape
    size = date_dev * 2 * row_count
    block_rows = size + 2 * (row_count // HALF) * date_dev
    return pl.pallas_call(
        functools.partial(pack_kernel, date_dev, row_count),
        out_shape=jax.ShapeDtypeStruct((devices, block_rows, LANES), BF16),
        in_specs=[pl.BlockSpec(memory_space=pltpu.VMEM)],
        out_specs=pl.BlockSpec(memory_space=pltpu.VMEM),
        scratch_shapes=[pltpu.VMEM((size, col_total), BF16)],
        compiler_params=pltpu.CompilerParams(vmem_limit_bytes=8 * size * col_total + 2**22),
        name="pack",
    )(tiles.reshape(size, col_total))


def remove_kernel(pixels, square_sum, series_ref, sums_ref, more_ref, coord_ref, out_ref, out_s, sems):
    dates = sums_ref.shape[1]
    eye = iota2((dates, dates), 0) == iota2((dates, dates), 1)
    sums = sums_ref[...]
    for i in range(more_ref.shape[0]):
        sums = sums + more_ref[i]
    mean = jnp.sum(jnp.where(eye, sums[0:1], 0.0), axis=1, keepdims=True) / pixels
    slope = jnp.sum(jnp.where(eye, sums[1:2], 0.0), axis=1, keepdims=True) / square_sum
    trend = mean + slope * coord_ref[...]
    rows = series_ref.shape[0] // dates
    chunks = sems.shape[0]
    per_chunk = dates // chunks
    copies = []
    for i in range(chunks):
        for d in range(i * per_chunk, (i + 1) * per_chunk):
            at = pl.ds(d * rows, rows)
            out_s[at, :] = series_ref[at, :] - trend[d : d + 1]
        at = pl.ds(i * per_chunk * rows, per_chunk * rows)
        copies.append(pltpu.make_async_copy(out_s.at[at], out_ref.at[at], sems.at[i]))
        copies[-1].start()
    for copy in copies:
        copy.wait()


def remove_trend(series, sums, more, coord, pixels, square_sum):
    chunks = 8
    return pl.pallas_call(
        functools.partial(remove_kernel, pixels, square_sum),
        out_shape=jax.ShapeDtypeStruct(series.shape, F32),
        in_specs=[pl.BlockSpec(memory_space=pltpu.VMEM)] * 4,
        out_specs=pl.BlockSpec(memory_space=pl.ANY),
        scratch_shapes=[pltpu.VMEM(series.shape, F32), pltpu.SemaphoreType.DMA((chunks,))],
        compiler_params=pltpu.CompilerParams(vmem_limit_bytes=8 * series.size + 2**22),
        name="remove",
    )(series, sums, more, coord)


def solve_matrix(pair_list, date_total):
    first, lag = pair_list[:, 0], pair_list[:, 1] - pair_list[:, 0]
    dates = lax.iota(jnp.int32, date_total)
    at_first = (dates[:, None] == first[None, :]).astype(F32)
    at_second = (dates[:, None] == pair_list[None, :, 1]).astype(F32)
    incidence = (at_first - at_second).astype(BF16)
    normal_matrix = jnp.dot(incidence, incidence.T, preferred_element_type=F32) + jnp.eye(date_total, dtype=F32)
    factor = jnp.linalg.cholesky(normal_matrix)
    lags = lax.iota(jnp.int32, LAGS) + 1
    at_lag = (lags[:, None] == lag[None, :]).astype(BF16)
    count = jnp.dot(at_lag, at_first.astype(BF16).T, preferred_element_type=F32)
    second = dates[None, :] + lags[:, None]
    ends = (dates[:, None, None] == dates[None, None, :]).astype(F32) - (
        dates[:, None, None] == second[None]
    ).astype(F32)
    columns = ends * count[None]
    units = date_total // SUB
    columns = columns.reshape(date_total, LAGS, units, SUB).transpose(0, 2, 1, 3).reshape(date_total, LAGS * date_total)
    solved = jax.scipy.linalg.cho_solve((factor, True), columns)
    return jnp.concatenate(split2(solved), axis=0)


def body(slc_tiles, look_weight, pair_list):
    devices = lax.axis_size("gx")
    position = lax.axis_index("gx")
    date_dev, _, row_count, col_total = slc_tiles.shape
    strip = col_total // devices
    date_total = date_dev * devices
    halves = row_count // HALF

    blocks = lax.all_to_all(pack(slc_tiles, devices), "gx", 0, 0, tiled=True)

    weight = lax.dynamic_slice_in_dim(look_weight, position * strip, strip, 1)
    weight_pad = jnp.pad(look_weight, ((0, 0), (RIM, RIM)))
    edge_weight = jnp.concatenate(
        [
            lax.dynamic_slice_in_dim(weight_pad, position * strip, RIM, 1),
            lax.dynamic_slice_in_dim(weight_pad, position * strip + strip + RIM, RIM, 1),
        ],
        axis=1,
    ).reshape(halves, LANES)
    solve = solve_matrix(pair_list, date_total)
    column_ids = position * strip + lax.iota(jnp.int32, strip)
    columns = (2.0 * column_ids.astype(F32) + 1.0) / col_total - 1.0

    series, sums = observe_all(blocks, weight, edge_weight, solve, columns[None], row_count, date_dev)
    rounds = []
    step = devices
    while step > 1:
        width = 4 if step % 4 == 0 else 2
        step //= width
        rounds.append([step * k for k in range(1, width)])
    for i, round_ in enumerate(rounds):
        parts = [lax.ppermute(sums, "gx", [(s, s ^ k) for s in range(devices)]) for k in round_]
        if i + 1 < len(rounds):
            for part in parts:
                sums = sums + part
    square_sum = row_count * (col_total * col_total - 1) / (3 * col_total)
    out = remove_trend(series, sums, jnp.stack(parts), columns[None], float(row_count * col_total), square_sum)
    return out.reshape(date_total, row_count, strip)


def solution(mesh):
    return jax.shard_map(
        body,
        mesh=mesh,
        in_specs=(P("gx", None, "band", None), P("band", None), P()),
        out_specs=P(None, "band", "gx"),
        check_vma=False,
    )
```

```python
import functools

import jax
import jax.numpy as jnp
from jax import lax
from jax.experimental import pallas as pl
from jax.experimental.pallas import tpu as pltpu
from jax.sharding import PartitionSpec as P

LOOK = 9
RIM = LOOK // 2
LAGS = 4
SUB = 8
LANES = 128
EDGE = 2 * RIM
HALF = LANES // EDGE

F32 = jnp.float32
BF16 = jnp.bfloat16


def iota2(shape, dim):
    return lax.broadcasted_iota(jnp.int32, shape, dim)


def split2(value):
    high = value.astype(BF16)
    low = (value - high.astype(F32)).astype(BF16)
    return high, low


def window_rows(rows, count):
    def add(a, b):
        return b if a is None else (a if b is None else a + b)

    def at(series, i):
        return series.get(i)

    base = {i: rows[i] for i in range(count)}
    two = {i: add(at(base, i), at(base, i + 1)) for i in range(-RIM, count)}
    four = {i: add(at(two, i), at(two, i + 2)) for i in range(-RIM, count)}
    eight = {i: add(at(four, i), at(four, i + 4)) for i in range(-RIM, count)}
    return [add(at(eight, r - RIM), at(base, r + RIM)) for r in range(count)]


def column_band():
    source = lax.rem(iota2((2 * LANES, LANES), 0), LANES)
    return (jnp.abs(source - iota2((2 * LANES, LANES), 1)) <= RIM).astype(BF16)


def edge_matrix(row_count):
    size = row_count * EDGE
    source, target = iota2((size, size), 0), iota2((size, size), 1)
    near = jnp.abs(source // EDGE - target // EDGE) <= RIM
    e, t = source % EDGE, target % EDGE
    left = (e < RIM) & (t >= RIM) & (e >= t - RIM)
    right = (e >= RIM) & (t < RIM) & (t >= e - RIM)
    return (near & (left | right)).astype(BF16)


def observe_kernel(
    row_count, unit_count,
    first_ref, next_ref, weight_ref, edge_weight_ref, band_ref, edge_ref, solve_ref, coord_ref,
    series_ref, sums_ref,
    re_s, im_s, wre_s, wim_s, pw_s, hre_s, him_s, hwre_s, hwim_s, obs_s,
):
    unit = pl.program_id(0)
    slots = (unit_count + 1) * SUB
    halves = row_count // HALF
    per_unit, block_rows, _ = next_ref.shape
    date_dev = SUB // per_unit
    hbase = 2 * date_dev * row_count
    pad = series_ref.shape[0] // solve_ref.shape[0] * 2

    def place(group_ref, new):
        for s in range(per_unit):
            for d in range(date_dev):
                for c, dst in ((0, re_s), (1, im_s)):
                    start = (d * 2 + c) * row_count
                    values = group_ref[s, pl.ds(start, row_count), :].astype(F32)
                    for g in range(row_count // SUB):
                        at = pl.ds(g * SUB * slots + new + s * date_dev + d, SUB, stride=slots)
                        dst[at, :] = values[g * SUB : (g + 1) * SUB]
            edge = group_ref[s, pl.ds(hbase, 2 * halves * date_dev), :].astype(F32)
            for c, dst in ((0, hre_s), (1, him_s)):
                for h in range(halves):
                    start = (c * halves + h) * date_dev
                    dst[pl.ds(h * slots + new + s * date_dev, date_dev), :] = edge[start : start + date_dev]

    lane = iota2((SUB, LANES), 1)
    at_edge = (lane >= LANES - RIM) | (lane < RIM)

    def power(re, im, wre, wim, weights, count, new):
        out = []
        for r in range(count):
            at = pl.ds(r * slots + new, SUB)
            w = weights[pl.ds(r, 1), :]
            a_re, a_im = re[at, :], im[at, :]
            w_re, w_im = w * a_re, w * a_im
            wre[at, :] = w_re
            wim[at, :] = w_im
            out.append(w_re * a_re + w_im * a_im)
        return out

    def cross(re, im, wre, wim, count, lag, old):
        out = []
        for r in range(count):
            at, ahead = pl.ds(r * slots + old, SUB), pl.ds(r * slots + old + lag, SUB)
            out.append(wim[at, :] * re[ahead, :] - wre[at, :] * im[ahead, :])
        return out

    def at_edges(images):
        halo = jnp.concatenate([jnp.concatenate(image, axis=1) for image in images], axis=0)
        summed = jnp.dot(jnp.concatenate(split2(halo), axis=0), edge_ref[...], preferred_element_type=F32)
        return summed[: halo.shape[0]] + summed[halo.shape[0] :]

    def look(image, edges):
        rows = jnp.concatenate(window_rows(image, row_count), axis=0)
        summed = jnp.dot(jnp.concatenate(split2(rows), axis=1), band_ref[...], preferred_element_type=F32)
        out = []
        for r in range(row_count):
            tile = edges[:, (r // HALF) * LANES : (r // HALF + 1) * LANES]
            rolled = pltpu.roll(tile, (LANES - RIM - EDGE * (r % HALF)) % LANES, 1)
            out.append(summed[r * SUB : (r + 1) * SUB] + jnp.where(at_edge, rolled, 0.0))
        return out

    def bring(group_ref, new):
        place(group_ref, new)
        edges = at_edges([power(hre_s, him_s, hwre_s, hwim_s, edge_weight_ref, halves, new)])
        image = power(re_s, im_s, wre_s, wim_s, weight_ref, row_count, new)
        for r, value in enumerate(look(image, edges)):
            pw_s[pl.ds(r * slots + new, SUB), :] = value

    combos = unit_count * SUB * LAGS

    @pl.when(unit == 0)
    def _():
        bring(first_ref, pl.multiple_of(unit * SUB, SUB))

    old = pl.multiple_of(unit * SUB, SUB)
    @pl.when(unit < unit_count)
    def _():
        bring(next_ref, pl.multiple_of(old + SUB, SUB))

    edges = at_edges([cross(hre_s, him_s, hwre_s, hwim_s, halves, lag, old) for lag in range(1, LAGS + 1)])

    def observed(lag):
        image = cross(re_s, im_s, wre_s, wim_s, row_count, lag, old)
        out = []
        for r, value in enumerate(look(image, edges[(lag - 1) * SUB : lag * SUB])):
            p = pw_s[pl.ds(r * slots + old, SUB), :]
            q = pw_s[pl.ds(r * slots + old + lag, SUB), :]
            out.append(value * lax.rsqrt(p * q + 1e-06))
        return out

    for lag in range(1, LAGS + 1, 2):
        first, second = observed(lag), observed(lag + 1)
        for r in range(row_count):
            at = pl.multiple_of(r * combos + unit * (SUB * LAGS) + (lag - 1) * SUB, 2 * SUB)
            obs_s[pl.ds(at, 2 * SUB), :] = jnp.concatenate([first[r], second[r]], axis=0).astype(BF16)

    @pl.when(unit == unit_count - 1)
    def _():
        solve = solve_ref[...]
        date_total = solve.shape[0] // 2
        mean = jnp.zeros((date_total, LANES), F32)
        for r in range(0, row_count, 2):
            pair = [obs_s[pl.ds((r + i) * combos, combos), :] for i in range(2)]
            both = jnp.dot(solve, jnp.concatenate(pair, axis=1), preferred_element_type=F32)
            both = both[:date_total] + both[date_total:]
            for i in range(2):
                series = both[:, i * LANES : (i + 1) * LANES]
                for g in range(date_total // SUB):
                    at = pl.ds(g * SUB * pad + r + i, SUB, stride=pad)
                    series_ref[at, :] = series[g * SUB : (g + 1) * SUB]
                mean = mean + series
        eye = iota2((date_total, date_total), 0) == iota2((date_total, date_total), 1)
        for i, part in enumerate((mean, mean * coord_ref[...])):
            column = jnp.sum(part, axis=1, keepdims=True)
            sums_ref[pl.ds(i, 1), :] = jnp.sum(jnp.where(eye, column, 0.0), axis=0, keepdims=True)


def observe_all(blocks, weight, edge_weight, solve, coord, row_count, date_dev):
    per_unit = SUB // date_dev
    sources, block_rows, _ = blocks.shape
    unit_count = sources // per_unit
    date_total = unit_count * SUB
    combos = date_total * LAGS
    halves = row_count // HALF
    slots = (unit_count + 1) * SUB
    pad = row_count + SUB
    whole = lambda a: pl.BlockSpec(a.shape, lambda u: (0,) * a.ndim)
    band, edge = column_band(), edge_matrix(row_count)
    scratch = [pltpu.VMEM((row_count * slots, LANES), F32)] * 5
    scratch += [pltpu.VMEM((halves * slots, LANES), F32)] * 4
    scratch += [pltpu.VMEM((row_count * combos, LANES), BF16)]
    words = row_count * LANES * (5 * slots + combos // 2 + 3 * date_total) + date_total * LANES * combos // 64
    return pl.pallas_call(
        functools.partial(observe_kernel, row_count, unit_count),
        grid=(unit_count,),
        out_shape=(
            jax.ShapeDtypeStruct((date_total * pad, LANES), F32),
            jax.ShapeDtypeStruct((2, date_total), F32),
        ),
        in_specs=[
            pl.BlockSpec((per_unit, block_rows, LANES), lambda u: (0, 0, 0)),
            pl.BlockSpec((per_unit, block_rows, LANES), lambda u: (lax.rem(u + 1, unit_count), 0, 0)),
            whole(weight), whole(edge_weight), whole(band), whole(edge), whole(solve), whole(coord),
        ],
        out_specs=(
            pl.BlockSpec((date_total * pad, LANES), lambda u: (0, 0)),
            pl.BlockSpec((2, date_total), lambda u: (0, 0)),
        ),
        scratch_shapes=scratch,
        compiler_params=pltpu.CompilerParams(
            dimension_semantics=("arbitrary",), vmem_limit_bytes=min(4 * words + 2**23, 2**26 - 2**17)
        ),
        name="observe",
    )(blocks, blocks, weight, edge_weight, band, edge, solve, coord)


def pack_kernel(date_dev, row_count, tiles_ref, out_ref, tiles_s, copies_s, edge_s, in_sems, out_sems, edge_sem):
    strips = out_ref.shape[0]
    size, col_total = tiles_s.shape
    halves = row_count // HALF
    chunks = in_sems.shape[0]
    per_chunk = strips // chunks
    arrivals = []
    for i in range(chunks):
        at = pl.ds(i * per_chunk * LANES, per_chunk * LANES)
        arrivals.append(pltpu.make_async_copy(tiles_ref.at[:, at], tiles_s.at[:, at], in_sems.at[i]))
        arrivals[-1].start()
    source, lane = iota2((2 * LANES, LANES), 0), iota2((2 * LANES, LANES), 1) % EDGE
    spread = (lane == jnp.where(source < LANES, source - (LANES - RIM), source - LANES + RIM)) & (
        (source >= LANES) == (lane >= RIM)
    )
    spread = spread.astype(BF16)
    mask = iota2((size, LANES), 0) % HALF == iota2((size, LANES), 1) // EDGE
    out_rows = 2 * halves * date_dev
    target, row = iota2((out_rows, size), 0), iota2((out_rows, size), 1)
    same = (
        (target % date_dev == row // (2 * row_count))
        & (target // (halves * date_dev) == row // row_count % 2)
        & (target // date_dev % halves == row // HALF % halves)
    ).astype(BF16)
    nothing = jnp.zeros((size, LANES), BF16)
    departures = []
    done = 0
    for i in range(chunks):
        arrivals[i].wait()
        ready = (i + 1) * per_chunk
        for j in range(ready - per_chunk, ready):
            strip = tiles_s.at[:, pl.ds(j * LANES, LANES)]
            departures.append(pltpu.make_async_copy(strip, out_ref.at[j, pl.ds(0, size)], out_sems.at[j]))
            departures[-1].start()
        upto = ready if i + 1 == chunks else ready - 1
        for j in range(done, upto):
            before = tiles_s[:, (j - 1) * LANES : j * LANES] if j else nothing
            after = tiles_s[:, (j + 1) * LANES : (j + 2) * LANES] if j + 1 < strips else nothing
            copies = jnp.dot(jnp.concatenate([before, after], axis=1), spread, preferred_element_type=F32)
            copies_s[:, j * LANES : (j + 1) * LANES] = jnp.where(mask, copies, 0.0).astype(BF16)
        done = upto
    edge = jnp.dot(same, copies_s[...], preferred_element_type=F32).astype(BF16)
    for j in range(strips):
        edge_s[j] = edge[:, j * LANES : (j + 1) * LANES]
    departures.append(pltpu.make_async_copy(edge_s, out_ref.at[:, pl.ds(size, out_rows)], edge_sem.at[0]))
    departures[-1].start()
    for departure in departures:
        departure.wait()


def pack(tiles, devices):
    date_dev, _, row_count, col_total = tiles.shape
    size = date_dev * 2 * row_count
    block_rows = size + 2 * (row_count // HALF) * date_dev
    return pl.pallas_call(
        functools.partial(pack_kernel, date_dev, row_count),
        out_shape=jax.ShapeDtypeStruct((devices, block_rows, LANES), BF16),
        in_specs=[pl.BlockSpec(memory_space=pl.ANY)],
        out_specs=pl.BlockSpec(memory_space=pl.ANY),
        scratch_shapes=[
            pltpu.VMEM((size, col_total), BF16),
            pltpu.VMEM((size, col_total), BF16),
            pltpu.VMEM((devices, block_rows - size, LANES), BF16),
            pltpu.SemaphoreType.DMA((4,)),
            pltpu.SemaphoreType.DMA((devices,)),
            pltpu.SemaphoreType.DMA((1,)),
        ],
        name="pack",
    )(tiles.reshape(size, col_total))


def remove_kernel(pixels, square_sum, series_ref, sums_ref, more_ref, coord_ref, out_ref, out_s, sems):
    dates = sums_ref.shape[1]
    eye = iota2((dates, dates), 0) == iota2((dates, dates), 1)
    sums = sums_ref[...]
    for i in range(more_ref.shape[0]):
        sums = sums + more_ref[i]
    mean = jnp.sum(jnp.where(eye, sums[0:1], 0.0), axis=1, keepdims=True) / pixels
    slope = jnp.sum(jnp.where(eye, sums[1:2], 0.0), axis=1, keepdims=True) / square_sum
    trend = mean + slope * coord_ref[...]
    pad, rows = series_ref.shape[0] // dates, out_ref.shape[0] // dates
    chunks = sems.shape[0]
    per_chunk = dates // chunks
    copies = []
    for i in range(chunks):
        for d in range(i * per_chunk, (i + 1) * per_chunk):
            out_s[pl.ds(d * rows, rows), :] = series_ref[pl.ds(d * pad, rows), :] - trend[d : d + 1]
        at = pl.ds(i * per_chunk * rows, per_chunk * rows)
        copies.append(pltpu.make_async_copy(out_s.at[at], out_ref.at[at], sems.at[i]))
        copies[-1].start()
    for copy in copies:
        copy.wait()


def remove_trend(series, sums, more, coord, rows, pixels, square_sum):
    chunks = 8
    return pl.pallas_call(
        functools.partial(remove_kernel, pixels, square_sum),
        out_shape=jax.ShapeDtypeStruct((rows, LANES), F32),
        in_specs=[pl.BlockSpec(memory_space=pltpu.VMEM)] * 4,
        out_specs=pl.BlockSpec(memory_space=pl.ANY),
        scratch_shapes=[pltpu.VMEM((rows, LANES), F32), pltpu.SemaphoreType.DMA((chunks,))],
        compiler_params=pltpu.CompilerParams(vmem_limit_bytes=8 * series.size + 2**22),
        name="remove",
    )(series, sums, more, coord)


def solve_matrix(pair_list, date_total):
    first, lag = pair_list[:, 0], pair_list[:, 1] - pair_list[:, 0]
    dates = lax.iota(jnp.int32, date_total)
    at_first = (dates[:, None] == first[None, :]).astype(F32)
    at_second = (dates[:, None] == pair_list[None, :, 1]).astype(F32)
    incidence = (at_first - at_second).astype(BF16)
    normal_matrix = jnp.dot(incidence, incidence.T, preferred_element_type=F32) + jnp.eye(date_total, dtype=F32)
    factor = jnp.linalg.cholesky(normal_matrix)
    lags = lax.iota(jnp.int32, LAGS) + 1
    at_lag = (lags[:, None] == lag[None, :]).astype(BF16)
    count = jnp.dot(at_lag, at_first.astype(BF16).T, preferred_element_type=F32)
    second = dates[None, :] + lags[:, None]
    ends = (dates[:, None, None] == dates[None, None, :]).astype(F32) - (
        dates[:, None, None] == second[None]
    ).astype(F32)
    columns = ends * count[None]
    units = date_total // SUB
    columns = columns.reshape(date_total, LAGS, units, SUB).transpose(0, 2, 1, 3).reshape(date_total, LAGS * date_total)
    solved = jax.scipy.linalg.cho_solve((factor, True), columns)
    return jnp.concatenate(split2(solved), axis=0)


def body(slc_tiles, look_weight, pair_list):
    devices = lax.axis_size("gx")
    position = lax.axis_index("gx")
    date_dev, _, row_count, col_total = slc_tiles.shape
    strip = col_total // devices
    date_total = date_dev * devices
    halves = row_count // HALF

    blocks = lax.all_to_all(pack(slc_tiles, devices), "gx", 0, 0, tiled=True)

    weight = lax.dynamic_slice_in_dim(look_weight, position * strip, strip, 1)
    weight_pad = jnp.pad(look_weight, ((0, 0), (RIM, RIM)))
    edge_weight = jnp.concatenate(
        [
            lax.dynamic_slice_in_dim(weight_pad, position * strip, RIM, 1),
            lax.dynamic_slice_in_dim(weight_pad, position * strip + strip + RIM, RIM, 1),
        ],
        axis=1,
    ).reshape(halves, LANES)
    solve = solve_matrix(pair_list, date_total)
    column_ids = position * strip + lax.iota(jnp.int32, strip)
    columns = (2.0 * column_ids.astype(F32) + 1.0) / col_total - 1.0

    series, sums = observe_all(blocks, weight, edge_weight, solve, columns[None], row_count, date_dev)
    rounds = []
    step = devices
    while step > 1:
        width = 4 if step % 4 == 0 else 2
        step //= width
        rounds.append([step * k for k in range(1, width)])
    for i, round_ in enumerate(rounds):
        parts = [lax.ppermute(sums, "gx", [(s, s ^ k) for s in range(devices)]) for k in round_]
        if i + 1 < len(rounds):
            for part in parts:
                sums = sums + part
    square_sum = row_count * (col_total * col_total - 1) / (3 * col_total)
    rows = date_total * row_count
    out = remove_trend(series, sums, jnp.stack(parts), columns[None], rows, float(row_count * col_total), square_sum)
    return out.reshape(date_total, row_count, strip)


def solution(mesh):
    return jax.shard_map(
        body,
        mesh=mesh,
        in_specs=(P("gx", None, "band", None), P("band", None), P()),
        out_specs=P(None, "band", "gx"),
        check_vma=False,
    )
```

```python
import functools

import jax
import jax.numpy as jnp
from jax import lax
from jax.experimental import pallas as pl
from jax.experimental.pallas import tpu as pltpu
from jax.sharding import PartitionSpec as P

LOOK = 9
RIM = LOOK // 2
LAGS = 4
SUB = 8
LANES = 128
EDGE = 2 * RIM
HALF = LANES // EDGE

F32 = jnp.float32
BF16 = jnp.bfloat16


def iota2(shape, dim):
    return lax.broadcasted_iota(jnp.int32, shape, dim)


def split2(value):
    high = value.astype(BF16)
    low = (value - high.astype(F32)).astype(BF16)
    return high, low


def window_rows(rows, count):
    def add(a, b):
        return b if a is None else (a if b is None else a + b)

    def at(series, i):
        return series.get(i)

    base = {i: rows[i] for i in range(count)}
    two = {i: add(at(base, i), at(base, i + 1)) for i in range(-RIM, count)}
    four = {i: add(at(two, i), at(two, i + 2)) for i in range(-RIM, count)}
    eight = {i: add(at(four, i), at(four, i + 4)) for i in range(-RIM, count)}
    return [add(at(eight, r - RIM), at(base, r + RIM)) for r in range(count)]


def column_band():
    source = lax.rem(iota2((2 * LANES, LANES), 0), LANES)
    return (jnp.abs(source - iota2((2 * LANES, LANES), 1)) <= RIM).astype(BF16)


def edge_matrix(row_count):
    size = row_count * EDGE
    source, target = iota2((size, size), 0), iota2((size, size), 1)
    near = jnp.abs(source // EDGE - target // EDGE) <= RIM
    e, t = source % EDGE, target % EDGE
    left = (e < RIM) & (t >= RIM) & (e >= t - RIM)
    right = (e >= RIM) & (t < RIM) & (t >= e - RIM)
    return (near & (left | right)).astype(BF16)


def observe_kernel(
    row_count, unit_count,
    blocks_ref, weight_ref, edge_weight_ref, band_ref, edge_ref, solve_ref, coord_ref,
    series_ref, sums_ref,
    re_s, im_s, wre_s, wim_s, pw_s, hre_s, him_s, hwre_s, hwim_s, obs_s,
):
    slots = (unit_count + 3) * SUB
    halves = row_count // HALF
    sources = blocks_ref.shape[0]
    per_unit = sources // unit_count
    date_dev = SUB // per_unit
    hbase = 2 * date_dev * row_count
    pad = series_ref.shape[0] // solve_ref.shape[0] * 2

    def place(group, new):
        for s in range(per_unit):
            source = group * per_unit + s
            for d in range(date_dev):
                for c, dst in ((0, re_s), (1, im_s)):
                    start = (d * 2 + c) * row_count
                    values = blocks_ref[source, pl.ds(start, row_count), :].astype(F32)
                    for g in range(row_count // SUB):
                        at = pl.ds(g * SUB * slots + new + s * date_dev + d, SUB, stride=slots)
                        dst[at, :] = values[g * SUB : (g + 1) * SUB]
            edge = blocks_ref[source, pl.ds(hbase, 2 * halves * date_dev), :].astype(F32)
            for c, dst in ((0, hre_s), (1, him_s)):
                for h in range(halves):
                    start = (c * halves + h) * date_dev
                    dst[pl.ds(h * slots + new + s * date_dev, date_dev), :] = edge[start : start + date_dev]

    lane = iota2((SUB, LANES), 1)
    at_edge = (lane >= LANES - RIM) | (lane < RIM)

    def power(re, im, wre, wim, weights, count, new):
        out = []
        for r in range(count):
            at = pl.ds(r * slots + new, SUB)
            w = weights[pl.ds(r, 1), :]
            a_re, a_im = re[at, :], im[at, :]
            w_re, w_im = w * a_re, w * a_im
            wre[at, :] = w_re
            wim[at, :] = w_im
            out.append(w_re * a_re + w_im * a_im)
        return out

    def cross(re, im, wre, wim, count, lag, old):
        out = []
        for r in range(count):
            at, ahead = pl.ds(r * slots + old, SUB), pl.ds(r * slots + old + lag, SUB)
            out.append(wim[at, :] * re[ahead, :] - wre[at, :] * im[ahead, :])
        return out

    def at_edges(images):
        halo = jnp.concatenate([jnp.concatenate(image, axis=1) for image in images], axis=0)
        summed = jnp.dot(jnp.concatenate(split2(halo), axis=0), edge_ref[...], preferred_element_type=F32)
        return summed[: halo.shape[0]] + summed[halo.shape[0] :]

    def look(image, edges):
        rows = jnp.concatenate(window_rows(image, row_count), axis=0)
        summed = jnp.dot(jnp.concatenate(split2(rows), axis=1), band_ref[...], preferred_element_type=F32)
        out = []
        for r in range(row_count):
            tile = edges[:, (r // HALF) * LANES : (r // HALF + 1) * LANES]
            rolled = pltpu.roll(tile, (LANES - RIM - EDGE * (r % HALF)) % LANES, 1)
            out.append(summed[r * SUB : (r + 1) * SUB] + jnp.where(at_edge, rolled, 0.0))
        return out

    def bring(group, new):
        place(lax.rem(group, unit_count), new)
        edges = at_edges([power(hre_s, him_s, hwre_s, hwim_s, edge_weight_ref, halves, new)])
        image = power(re_s, im_s, wre_s, wim_s, weight_ref, row_count, new)
        for r, value in enumerate(look(image, edges)):
            pw_s[pl.ds(r * slots + new, SUB), :] = value

    combos = unit_count * SUB * LAGS

    together = 3 if (unit_count + 1) % 3 == 0 else 2

    def bring_some(step, carry):
        for g in range(together):
            bring(together * step + g, pl.multiple_of((together * step + g) * SUB, SUB))
        return carry

    lax.fori_loop(0, -(-(unit_count + 1) // together), bring_some, 0)

    def observe_unit(unit, carry):
        old = pl.multiple_of(unit * SUB, SUB)
        edges = at_edges([cross(hre_s, him_s, hwre_s, hwim_s, halves, lag, old) for lag in range(1, LAGS + 1)])

        def observed(lag):
            image = cross(re_s, im_s, wre_s, wim_s, row_count, lag, old)
            out = []
            for r, value in enumerate(look(image, edges[(lag - 1) * SUB : lag * SUB])):
                p = pw_s[pl.ds(r * slots + old, SUB), :]
                q = pw_s[pl.ds(r * slots + old + lag, SUB), :]
                out.append(value * lax.rsqrt(p * q + 1e-06))
            return out

        for lag in range(1, LAGS + 1, 2):
            first, second = observed(lag), observed(lag + 1)
            for r in range(row_count):
                at = pl.multiple_of(r * combos + unit * (SUB * LAGS) + (lag - 1) * SUB, 2 * SUB)
                obs_s[pl.ds(at, 2 * SUB), :] = jnp.concatenate([first[r], second[r]], axis=0).astype(BF16)
        return carry

    lax.fori_loop(0, unit_count, observe_unit, 0)

    solve = solve_ref[...]
    date_total = solve.shape[0] // 2
    mean = jnp.zeros((date_total, LANES), F32)
    for r in range(0, row_count, 2):
        pair = [obs_s[pl.ds((r + i) * combos, combos), :] for i in range(2)]
        both = jnp.dot(solve, jnp.concatenate(pair, axis=1), preferred_element_type=F32)
        both = both[:date_total] + both[date_total:]
        for i in range(2):
            series = both[:, i * LANES : (i + 1) * LANES]
            for g in range(date_total // SUB):
                at = pl.ds(g * SUB * pad + r + i, SUB, stride=pad)
                series_ref[at, :] = series[g * SUB : (g + 1) * SUB]
            mean = mean + series
    eye = iota2((date_total, date_total), 0) == iota2((date_total, date_total), 1)
    for i, part in enumerate((mean, mean * coord_ref[...])):
        column = jnp.sum(part, axis=1, keepdims=True)
        sums_ref[pl.ds(i, 1), :] = jnp.sum(jnp.where(eye, column, 0.0), axis=0, keepdims=True)


def observe_all(blocks, weight, edge_weight, solve, coord, row_count, date_dev):
    per_unit = SUB // date_dev
    sources, block_rows, _ = blocks.shape
    unit_count = sources // per_unit
    date_total = unit_count * SUB
    combos = date_total * LAGS
    halves = row_count // HALF
    slots = (unit_count + 3) * SUB
    pad = row_count + SUB
    band, edge = column_band(), edge_matrix(row_count)
    scratch = [pltpu.VMEM((row_count * slots, LANES), F32)] * 5
    scratch += [pltpu.VMEM((halves * slots, LANES), F32)] * 4
    scratch += [pltpu.VMEM((row_count * combos, LANES), BF16)]
    words = row_count * LANES * (5 * slots + combos // 2 + 3 * date_total) + date_total * LANES * combos // 64
    return pl.pallas_call(
        functools.partial(observe_kernel, row_count, unit_count),
        out_shape=(
            jax.ShapeDtypeStruct((date_total * pad, LANES), F32),
            jax.ShapeDtypeStruct((2, date_total), F32),
        ),
        in_specs=[pl.BlockSpec(memory_space=pltpu.VMEM)] * 7,
        out_specs=[pl.BlockSpec(memory_space=pltpu.VMEM)] * 2,
        scratch_shapes=scratch,
        compiler_params=pltpu.CompilerParams(vmem_limit_bytes=min(4 * words + 2**23, 2**26 - 2**17)),
        name="observe",
    )(blocks, weight, edge_weight, band, edge, solve, coord)


def pack_kernel(date_dev, row_count, tiles_ref, out_ref, tiles_s, copies_s, edge_s, in_sems, out_sems, edge_sem):
    strips = out_ref.shape[0]
    size, col_total = tiles_s.shape
    halves = row_count // HALF
    chunks = in_sems.shape[0]
    per_chunk = strips // chunks
    arrivals = []
    for i in range(chunks):
        at = pl.ds(i * per_chunk * LANES, per_chunk * LANES)
        arrivals.append(pltpu.make_async_copy(tiles_ref.at[:, at], tiles_s.at[:, at], in_sems.at[i]))
        arrivals[-1].start()
    source, lane = iota2((2 * LANES, LANES), 0), iota2((2 * LANES, LANES), 1) % EDGE
    spread = (lane == jnp.where(source < LANES, source - (LANES - RIM), source - LANES + RIM)) & (
        (source >= LANES) == (lane >= RIM)
    )
    spread = spread.astype(BF16)
    mask = iota2((size, LANES), 0) % HALF == iota2((size, LANES), 1) // EDGE
    out_rows = 2 * halves * date_dev
    target, row = iota2((out_rows, size), 0), iota2((out_rows, size), 1)
    same = (
        (target % date_dev == row // (2 * row_count))
        & (target // (halves * date_dev) == row // row_count % 2)
        & (target // date_dev % halves == row // HALF % halves)
    ).astype(BF16)
    nothing = jnp.zeros((size, LANES), BF16)
    departures = []
    done = 0
    for i in range(chunks):
        arrivals[i].wait()
        ready = (i + 1) * per_chunk
        for j in range(ready - per_chunk, ready):
            strip = tiles_s.at[:, pl.ds(j * LANES, LANES)]
            departures.append(pltpu.make_async_copy(strip, out_ref.at[j, pl.ds(0, size)], out_sems.at[j]))
            departures[-1].start()
        upto = ready if i + 1 == chunks else ready - 1
        for j in range(done, upto):
            before = tiles_s[:, (j - 1) * LANES : j * LANES] if j else nothing
            after = tiles_s[:, (j + 1) * LANES : (j + 2) * LANES] if j + 1 < strips else nothing
            copies = jnp.dot(jnp.concatenate([before, after], axis=1), spread, preferred_element_type=F32)
            copies_s[:, j * LANES : (j + 1) * LANES] = jnp.where(mask, copies, 0.0).astype(BF16)
        done = upto
    edge = jnp.dot(same, copies_s[...], preferred_element_type=F32).astype(BF16)
    for j in range(strips):
        edge_s[j] = edge[:, j * LANES : (j + 1) * LANES]
    departures.append(pltpu.make_async_copy(edge_s, out_ref.at[:, pl.ds(size, out_rows)], edge_sem.at[0]))
    departures[-1].start()
    for departure in departures:
        departure.wait()


def pack(tiles, devices):
    date_dev, _, row_count, col_total = tiles.shape
    size = date_dev * 2 * row_count
    block_rows = size + 2 * (row_count // HALF) * date_dev
    return pl.pallas_call(
        functools.partial(pack_kernel, date_dev, row_count),
        out_shape=jax.ShapeDtypeStruct((devices, block_rows, LANES), BF16),
        in_specs=[pl.BlockSpec(memory_space=pl.ANY)],
        out_specs=pl.BlockSpec(memory_space=pl.ANY),
        scratch_shapes=[
            pltpu.VMEM((size, col_total), BF16),
            pltpu.VMEM((size, col_total), BF16),
            pltpu.VMEM((devices, block_rows - size, LANES), BF16),
            pltpu.SemaphoreType.DMA((4,)),
            pltpu.SemaphoreType.DMA((devices,)),
            pltpu.SemaphoreType.DMA((1,)),
        ],
        name="pack",
    )(tiles.reshape(size, col_total))


def remove_kernel(pixels, square_sum, series_ref, sums_ref, more_ref, coord_ref, out_ref, out_s, sems):
    dates = sums_ref.shape[1]
    eye = iota2((dates, dates), 0) == iota2((dates, dates), 1)
    sums = sums_ref[...]
    for i in range(more_ref.shape[0]):
        sums = sums + more_ref[i]
    mean = jnp.sum(jnp.where(eye, sums[0:1], 0.0), axis=1, keepdims=True) / pixels
    slope = jnp.sum(jnp.where(eye, sums[1:2], 0.0), axis=1, keepdims=True) / square_sum
    trend = mean + slope * coord_ref[...]
    pad, rows = series_ref.shape[0] // dates, out_ref.shape[0] // dates
    chunks = sems.shape[0]
    per_chunk = dates // chunks
    copies = []
    for i in range(chunks):
        for d in range(i * per_chunk, (i + 1) * per_chunk):
            out_s[pl.ds(d * rows, rows), :] = series_ref[pl.ds(d * pad, rows), :] - trend[d : d + 1]
        at = pl.ds(i * per_chunk * rows, per_chunk * rows)
        copies.append(pltpu.make_async_copy(out_s.at[at], out_ref.at[at], sems.at[i]))
        copies[-1].start()
    for copy in copies:
        copy.wait()


def remove_trend(series, sums, more, coord, rows, pixels, square_sum):
    chunks = 8
    return pl.pallas_call(
        functools.partial(remove_kernel, pixels, square_sum),
        out_shape=jax.ShapeDtypeStruct((rows, LANES), F32),
        in_specs=[pl.BlockSpec(memory_space=pltpu.VMEM)] * 4,
        out_specs=pl.BlockSpec(memory_space=pl.ANY),
        scratch_shapes=[pltpu.VMEM((rows, LANES), F32), pltpu.SemaphoreType.DMA((chunks,))],
        compiler_params=pltpu.CompilerParams(vmem_limit_bytes=8 * series.size + 2**22),
        name="remove",
    )(series, sums, more, coord)


def solve_matrix(pair_list, date_total):
    first, lag = pair_list[:, 0], pair_list[:, 1] - pair_list[:, 0]
    dates = lax.iota(jnp.int32, date_total)
    at_first = (dates[:, None] == first[None, :]).astype(F32)
    at_second = (dates[:, None] == pair_list[None, :, 1]).astype(F32)
    incidence = (at_first - at_second).astype(BF16)
    normal_matrix = jnp.dot(incidence, incidence.T, preferred_element_type=F32) + jnp.eye(date_total, dtype=F32)
    factor = jnp.linalg.cholesky(normal_matrix)
    lags = lax.iota(jnp.int32, LAGS) + 1
    at_lag = (lags[:, None] == lag[None, :]).astype(BF16)
    count = jnp.dot(at_lag, at_first.astype(BF16).T, preferred_element_type=F32)
    second = dates[None, :] + lags[:, None]
    ends = (dates[:, None, None] == dates[None, None, :]).astype(F32) - (
        dates[:, None, None] == second[None]
    ).astype(F32)
    columns = ends * count[None]
    units = date_total // SUB
    columns = columns.reshape(date_total, LAGS, units, SUB).transpose(0, 2, 1, 3).reshape(date_total, LAGS * date_total)
    solved = jax.scipy.linalg.cho_solve((factor, True), columns)
    return jnp.concatenate(split2(solved), axis=0)


def body(slc_tiles, look_weight, pair_list):
    devices = lax.axis_size("gx")
    position = lax.axis_index("gx")
    date_dev, _, row_count, col_total = slc_tiles.shape
    strip = col_total // devices
    date_total = date_dev * devices
    halves = row_count // HALF

    blocks = lax.all_to_all(pack(slc_tiles, devices), "gx", 0, 0, tiled=True)

    weight = lax.dynamic_slice_in_dim(look_weight, position * strip, strip, 1)
    weight_pad = jnp.pad(look_weight, ((0, 0), (RIM, RIM)))
    edge_weight = jnp.concatenate(
        [
            lax.dynamic_slice_in_dim(weight_pad, position * strip, RIM, 1),
            lax.dynamic_slice_in_dim(weight_pad, position * strip + strip + RIM, RIM, 1),
        ],
        axis=1,
    ).reshape(halves, LANES)
    solve = solve_matrix(pair_list, date_total)
    column_ids = position * strip + lax.iota(jnp.int32, strip)
    columns = (2.0 * column_ids.astype(F32) + 1.0) / col_total - 1.0

    series, sums = observe_all(blocks, weight, edge_weight, solve, columns[None], row_count, date_dev)
    rounds = []
    step = devices
    while step > 1:
        width = 4 if step % 4 == 0 else 2
        step //= width
        rounds.append([step * k for k in range(1, width)])
    for i, round_ in enumerate(rounds):
        parts = [lax.ppermute(sums, "gx", [(s, s ^ k) for s in range(devices)]) for k in round_]
        if i + 1 < len(rounds):
            for part in parts:
                sums = sums + part
    square_sum = row_count * (col_total * col_total - 1) / (3 * col_total)
    rows = date_total * row_count
    out = remove_trend(series, sums, jnp.stack(parts), columns[None], rows, float(row_count * col_total), square_sum)
    return out.reshape(date_total, row_count, strip)


def solution(mesh):
    return jax.shard_map(
        body,
        mesh=mesh,
        in_specs=(P("gx", None, "band", None), P("band", None), P()),
        out_specs=P(None, "band", "gx"),
        check_vma=False,
    )
```

```python
import functools

import jax
import jax.numpy as jnp
from jax import lax
from jax.experimental import pallas as pl
from jax.experimental.pallas import tpu as pltpu
from jax.sharding import PartitionSpec as P

LOOK = 9
RIM = LOOK // 2
LAGS = 4
SUB = 8
LANES = 128
EDGE = 2 * RIM
HALF = LANES // EDGE

F32 = jnp.float32
BF16 = jnp.bfloat16


def iota2(shape, dim):
    return lax.broadcasted_iota(jnp.int32, shape, dim)


def split2(value):
    high = value.astype(BF16)
    low = (value - high.astype(F32)).astype(BF16)
    return high, low


def window_rows(rows, count):
    def add(a, b):
        return b if a is None else (a if b is None else a + b)

    def at(series, i):
        return series.get(i)

    base = {i: rows[i] for i in range(count)}
    two = {i: add(at(base, i), at(base, i + 1)) for i in range(-RIM, count)}
    four = {i: add(at(two, i), at(two, i + 2)) for i in range(-RIM, count)}
    eight = {i: add(at(four, i), at(four, i + 4)) for i in range(-RIM, count)}
    return [add(at(eight, r - RIM), at(base, r + RIM)) for r in range(count)]


def column_band():
    source = lax.rem(iota2((2 * LANES, LANES), 0), LANES)
    return (jnp.abs(source - iota2((2 * LANES, LANES), 1)) <= RIM).astype(BF16)


def edge_matrix(row_count):
    size = row_count * EDGE
    source, target = iota2((size, size), 0), iota2((size, size), 1)
    near = jnp.abs(source // EDGE - target // EDGE) <= RIM
    e, t = source % EDGE, target % EDGE
    left = (e < RIM) & (t >= RIM) & (e >= t - RIM)
    right = (e >= RIM) & (t < RIM) & (t >= e - RIM)
    return (near & (left | right)).astype(BF16)


def observe_kernel(
    row_count, unit_count,
    blocks_ref, weight_ref, edge_weight_ref, band_ref, edge_ref, solve_ref, coord_ref,
    series_ref, sums_ref,
    re_s, im_s, wre_s, wim_s, pw_s, hre_s, him_s, hwre_s, hwim_s, obs_s,
):
    slots = (unit_count + 3) * SUB
    halves = row_count // HALF
    sources = blocks_ref.shape[0]
    per_unit = sources // unit_count
    date_dev = SUB // per_unit
    hbase = 2 * date_dev * row_count
    pad = series_ref.shape[0] // solve_ref.shape[0] * 2

    def place(group, new):
        for s in range(per_unit):
            source = group * per_unit + s
            for d in range(date_dev):
                for c, dst in ((0, re_s), (1, im_s)):
                    start = (d * 2 + c) * row_count
                    values = blocks_ref[source, pl.ds(start, row_count), :].astype(F32)
                    for g in range(row_count // SUB):
                        at = pl.ds(g * SUB * slots + new + s * date_dev + d, SUB, stride=slots)
                        dst[at, :] = values[g * SUB : (g + 1) * SUB]
            edge = blocks_ref[source, pl.ds(hbase, 2 * halves * date_dev), :].astype(F32)
            for c, dst in ((0, hre_s), (1, him_s)):
                for h in range(halves):
                    start = (c * halves + h) * date_dev
                    dst[pl.ds(h * slots + new + s * date_dev, date_dev), :] = edge[start : start + date_dev]

    lane = iota2((SUB, LANES), 1)
    at_edge = (lane >= LANES - RIM) | (lane < RIM)

    def power(re, im, wre, wim, weights, count, new):
        out = []
        for r in range(count):
            at = pl.ds(r * slots + new, SUB)
            w = weights[pl.ds(r, 1), :]
            a_re, a_im = re[at, :], im[at, :]
            w_re, w_im = w * a_re, w * a_im
            wre[at, :] = w_re
            wim[at, :] = w_im
            out.append(w_re * a_re + w_im * a_im)
        return out

    def cross(re, im, wre, wim, count, lag, old):
        out = []
        for r in range(count):
            at, ahead = pl.ds(r * slots + old, SUB), pl.ds(r * slots + old + lag, SUB)
            out.append(wim[at, :] * re[ahead, :] - wre[at, :] * im[ahead, :])
        return out

    def at_edges(images):
        halo = jnp.concatenate([jnp.concatenate(image, axis=1) for image in images], axis=0)
        summed = jnp.dot(jnp.concatenate(split2(halo), axis=0), edge_ref[...], preferred_element_type=F32)
        return summed[: halo.shape[0]] + summed[halo.shape[0] :]

    def look(image, edges):
        rows = jnp.concatenate(window_rows(image, row_count), axis=0)
        summed = jnp.dot(jnp.concatenate(split2(rows), axis=1), band_ref[...], preferred_element_type=F32)
        out = []
        for r in range(row_count):
            tile = edges[:, (r // HALF) * LANES : (r // HALF + 1) * LANES]
            rolled = pltpu.roll(tile, (LANES - RIM - EDGE * (r % HALF)) % LANES, 1)
            out.append(summed[r * SUB : (r + 1) * SUB] + jnp.where(at_edge, rolled, 0.0))
        return out

    def bring(group, new):
        place(lax.rem(group, unit_count), new)
        edges = at_edges([power(hre_s, him_s, hwre_s, hwim_s, edge_weight_ref, halves, new)])
        image = power(re_s, im_s, wre_s, wim_s, weight_ref, row_count, new)
        for r, value in enumerate(look(image, edges)):
            pw_s[pl.ds(r * slots + new, SUB), :] = value

    combos = unit_count * SUB * LAGS

    together = 3 if (unit_count + 1) % 3 == 0 else 2

    def bring_some(step, carry):
        for g in range(together):
            bring(together * step + g, pl.multiple_of((together * step + g) * SUB, SUB))
        return carry

    lax.fori_loop(0, -(-(unit_count + 1) // together), bring_some, 0)

    def observe_unit(unit, carry):
        old = pl.multiple_of(unit * SUB, SUB)
        edges = at_edges([cross(hre_s, him_s, hwre_s, hwim_s, halves, lag, old) for lag in range(1, LAGS + 1)])

        def observed(lag):
            image = cross(re_s, im_s, wre_s, wim_s, row_count, lag, old)
            out = []
            for r, value in enumerate(look(image, edges[(lag - 1) * SUB : lag * SUB])):
                p = pw_s[pl.ds(r * slots + old, SUB), :]
                q = pw_s[pl.ds(r * slots + old + lag, SUB), :]
                out.append(value * lax.rsqrt(p * q + 1e-06))
            return out

        for lag in range(1, LAGS + 1, 2):
            first, second = observed(lag), observed(lag + 1)
            for r in range(row_count):
                at = pl.multiple_of(r * combos + unit * (SUB * LAGS) + (lag - 1) * SUB, 2 * SUB)
                obs_s[pl.ds(at, 2 * SUB), :] = jnp.concatenate([first[r], second[r]], axis=0).astype(BF16)
        return carry

    lax.fori_loop(0, unit_count, observe_unit, 0)

    solve = solve_ref[...]
    date_total = solve.shape[0] // 2
    mean = jnp.zeros((date_total, LANES), F32)
    for r in range(0, row_count, 2):
        pair = [obs_s[pl.ds((r + i) * combos, combos), :] for i in range(2)]
        both = jnp.dot(solve, jnp.concatenate(pair, axis=1), preferred_element_type=F32)
        both = both[:date_total] + both[date_total:]
        for i in range(2):
            series = both[:, i * LANES : (i + 1) * LANES]
            for g in range(date_total // SUB):
                at = pl.ds(g * SUB * pad + r + i, SUB, stride=pad)
                series_ref[at, :] = series[g * SUB : (g + 1) * SUB]
            mean = mean + series
    eye = iota2((date_total, date_total), 0) == iota2((date_total, date_total), 1)
    for i, part in enumerate((mean, mean * coord_ref[...])):
        column = jnp.sum(part, axis=1, keepdims=True)
        sums_ref[pl.ds(i, 1), :] = jnp.sum(jnp.where(eye, column, 0.0), axis=0, keepdims=True)


def observe_all(blocks, weight, edge_weight, solve, coord, row_count, date_dev):
    per_unit = SUB // date_dev
    sources, block_rows, _ = blocks.shape
    unit_count = sources // per_unit
    date_total = unit_count * SUB
    combos = date_total * LAGS
    halves = row_count // HALF
    slots = (unit_count + 3) * SUB
    pad = row_count + SUB
    band, edge = column_band(), edge_matrix(row_count)
    scratch = [pltpu.VMEM((row_count * slots, LANES), F32)] * 5
    scratch += [pltpu.VMEM((halves * slots, LANES), F32)] * 4
    scratch += [pltpu.VMEM((row_count * combos, LANES), BF16)]
    words = row_count * LANES * (5 * slots + combos // 2 + 3 * date_total) + date_total * LANES * combos // 64
    return pl.pallas_call(
        functools.partial(observe_kernel, row_count, unit_count),
        out_shape=(
            jax.ShapeDtypeStruct((date_total * pad, LANES), F32),
            jax.ShapeDtypeStruct((2, date_total), F32),
        ),
        in_specs=[pl.BlockSpec(memory_space=pltpu.VMEM)] * 7,
        out_specs=[pl.BlockSpec(memory_space=pltpu.VMEM)] * 2,
        scratch_shapes=scratch,
        compiler_params=pltpu.CompilerParams(vmem_limit_bytes=min(4 * words + 2**23, 2**26 - 2**17)),
        name="observe",
    )(blocks, weight, edge_weight, band, edge, solve, coord)


def pack_kernel(date_dev, row_count, tiles_ref, out_ref, tiles_s, copies_s, edge_s, in_sems, out_sems, edge_sem):
    strips = out_ref.shape[0]
    size, col_total = tiles_s.shape
    halves = row_count // HALF
    chunks = in_sems.shape[0]
    arrivals = []
    for i in range(chunks):
        at = pl.ds(i * (size // chunks), size // chunks)
        arrivals.append(pltpu.make_async_copy(tiles_ref.at[at], tiles_s.at[at], in_sems.at[i]))
        arrivals[-1].start()
    source, lane = iota2((2 * LANES, LANES), 0), iota2((2 * LANES, LANES), 1) % EDGE
    spread = (lane == jnp.where(source < LANES, source - (LANES - RIM), source - LANES + RIM)) & (
        (source >= LANES) == (lane >= RIM)
    )
    spread = spread.astype(BF16)
    mask = iota2((size, LANES), 0) % HALF == iota2((size, LANES), 1) // EDGE
    out_rows = 2 * halves * date_dev
    target, row = iota2((out_rows, size), 0), iota2((out_rows, size), 1)
    same = (
        (target % date_dev == row // (2 * row_count))
        & (target // (halves * date_dev) == row // row_count % 2)
        & (target // date_dev % halves == row // HALF % halves)
    ).astype(BF16)
    nothing = jnp.zeros((size, LANES), BF16)
    for arrival in arrivals:
        arrival.wait()
    departures = []
    for j in range(strips):
        strip = tiles_s.at[:, pl.ds(j * LANES, LANES)]
        departures.append(pltpu.make_async_copy(strip, out_ref.at[j, pl.ds(0, size)], out_sems.at[j]))
        departures[-1].start()
    for j in range(strips):
        before = tiles_s[:, (j - 1) * LANES : j * LANES] if j else nothing
        after = tiles_s[:, (j + 1) * LANES : (j + 2) * LANES] if j + 1 < strips else nothing
        copies = jnp.dot(jnp.concatenate([before, after], axis=1), spread, preferred_element_type=F32)
        copies_s[:, j * LANES : (j + 1) * LANES] = jnp.where(mask, copies, 0.0).astype(BF16)
    edge = jnp.dot(same, copies_s[...], preferred_element_type=F32).astype(BF16)
    for j in range(strips):
        edge_s[j] = edge[:, j * LANES : (j + 1) * LANES]
    departures.append(pltpu.make_async_copy(edge_s, out_ref.at[:, pl.ds(size, out_rows)], edge_sem.at[0]))
    departures[-1].start()
    for departure in departures:
        departure.wait()


def pack(tiles, devices):
    date_dev, _, row_count, col_total = tiles.shape
    size = date_dev * 2 * row_count
    block_rows = size + 2 * (row_count // HALF) * date_dev
    return pl.pallas_call(
        functools.partial(pack_kernel, date_dev, row_count),
        out_shape=jax.ShapeDtypeStruct((devices, block_rows, LANES), BF16),
        in_specs=[pl.BlockSpec(memory_space=pl.ANY)],
        out_specs=pl.BlockSpec(memory_space=pl.ANY),
        scratch_shapes=[
            pltpu.VMEM((size, col_total), BF16),
            pltpu.VMEM((size, col_total), BF16),
            pltpu.VMEM((devices, block_rows - size, LANES), BF16),
            pltpu.SemaphoreType.DMA((4,)),
            pltpu.SemaphoreType.DMA((devices,)),
            pltpu.SemaphoreType.DMA((1,)),
        ],
        name="pack",
    )(tiles.reshape(size, col_total))


def remove_kernel(pixels, square_sum, series_ref, sums_ref, more_ref, coord_ref, out_ref, out_s, sems):
    dates = sums_ref.shape[1]
    eye = iota2((dates, dates), 0) == iota2((dates, dates), 1)
    sums = sums_ref[...]
    for i in range(more_ref.shape[0]):
        sums = sums + more_ref[i]
    mean = jnp.sum(jnp.where(eye, sums[0:1], 0.0), axis=1, keepdims=True) / pixels
    slope = jnp.sum(jnp.where(eye, sums[1:2], 0.0), axis=1, keepdims=True) / square_sum
    trend = mean + slope * coord_ref[...]
    pad, rows = series_ref.shape[0] // dates, out_ref.shape[0] // dates
    chunks = sems.shape[0]
    per_chunk = dates // chunks
    copies = []
    for i in range(chunks):
        for d in range(i * per_chunk, (i + 1) * per_chunk):
            out_s[pl.ds(d * rows, rows), :] = series_ref[pl.ds(d * pad, rows), :] - trend[d : d + 1]
        at = pl.ds(i * per_chunk * rows, per_chunk * rows)
        copies.append(pltpu.make_async_copy(out_s.at[at], out_ref.at[at], sems.at[i]))
        copies[-1].start()
    for copy in copies:
        copy.wait()


def remove_trend(series, sums, more, coord, rows, pixels, square_sum):
    chunks = 8
    return pl.pallas_call(
        functools.partial(remove_kernel, pixels, square_sum),
        out_shape=jax.ShapeDtypeStruct((rows, LANES), F32),
        in_specs=[pl.BlockSpec(memory_space=pltpu.VMEM)] * 4,
        out_specs=pl.BlockSpec(memory_space=pl.ANY),
        scratch_shapes=[pltpu.VMEM((rows, LANES), F32), pltpu.SemaphoreType.DMA((chunks,))],
        compiler_params=pltpu.CompilerParams(vmem_limit_bytes=8 * series.size + 2**22),
        name="remove",
    )(series, sums, more, coord)


def solve_matrix(pair_list, date_total):
    first, lag = pair_list[:, 0], pair_list[:, 1] - pair_list[:, 0]
    dates = lax.iota(jnp.int32, date_total)
    at_first = (dates[:, None] == first[None, :]).astype(F32)
    at_second = (dates[:, None] == pair_list[None, :, 1]).astype(F32)
    incidence = (at_first - at_second).astype(BF16)
    normal_matrix = jnp.dot(incidence, incidence.T, preferred_element_type=F32) + jnp.eye(date_total, dtype=F32)
    factor = jnp.linalg.cholesky(normal_matrix)
    lags = lax.iota(jnp.int32, LAGS) + 1
    at_lag = (lags[:, None] == lag[None, :]).astype(BF16)
    count = jnp.dot(at_lag, at_first.astype(BF16).T, preferred_element_type=F32)
    second = dates[None, :] + lags[:, None]
    ends = (dates[:, None, None] == dates[None, None, :]).astype(F32) - (
        dates[:, None, None] == second[None]
    ).astype(F32)
    columns = ends * count[None]
    units = date_total // SUB
    columns = columns.reshape(date_total, LAGS, units, SUB).transpose(0, 2, 1, 3).reshape(date_total, LAGS * date_total)
    solved = jax.scipy.linalg.cho_solve((factor, True), columns)
    return jnp.concatenate(split2(solved), axis=0)


def body(slc_tiles, look_weight, pair_list):
    devices = lax.axis_size("gx")
    position = lax.axis_index("gx")
    date_dev, _, row_count, col_total = slc_tiles.shape
    strip = col_total // devices
    date_total = date_dev * devices
    halves = row_count // HALF

    blocks = lax.all_to_all(pack(slc_tiles, devices), "gx", 0, 0, tiled=True)

    weight = lax.dynamic_slice_in_dim(look_weight, position * strip, strip, 1)
    weight_pad = jnp.pad(look_weight, ((0, 0), (RIM, RIM)))
    edge_weight = jnp.concatenate(
        [
            lax.dynamic_slice_in_dim(weight_pad, position * strip, RIM, 1),
            lax.dynamic_slice_in_dim(weight_pad, position * strip + strip + RIM, RIM, 1),
        ],
        axis=1,
    ).reshape(halves, LANES)
    solve = solve_matrix(pair_list, date_total)
    column_ids = position * strip + lax.iota(jnp.int32, strip)
    columns = (2.0 * column_ids.astype(F32) + 1.0) / col_total - 1.0

    series, sums = observe_all(blocks, weight, edge_weight, solve, columns[None], row_count, date_dev)
    rounds = []
    step = devices
    while step > 1:
        width = 4 if step % 4 == 0 else 2
        step //= width
        rounds.append([step * k for k in range(1, width)])
    for i, round_ in enumerate(rounds):
        parts = [lax.ppermute(sums, "gx", [(s, s ^ k) for s in range(devices)]) for k in round_]
        if i + 1 < len(rounds):
            for part in parts:
                sums = sums + part
    square_sum = row_count * (col_total * col_total - 1) / (3 * col_total)
    rows = date_total * row_count
    out = remove_trend(series, sums, jnp.stack(parts), columns[None], rows, float(row_count * col_total), square_sum)
    return out.reshape(date_total, row_count, strip)


def solution(mesh):
    return jax.shard_map(
        body,
        mesh=mesh,
        in_specs=(P("gx", None, "band", None), P("band", None), P()),
        out_specs=P(None, "band", "gx"),
        check_vma=False,
    )
```

```python
import functools

import jax
import jax.numpy as jnp
from jax import lax
from jax.experimental import pallas as pl
from jax.experimental.pallas import tpu as pltpu
from jax.sharding import PartitionSpec as P

LOOK = 9
RIM = LOOK // 2
LAGS = 4
SUB = 8
LANES = 128
EDGE = 2 * RIM
HALF = LANES // EDGE

F32 = jnp.float32
BF16 = jnp.bfloat16


def iota2(shape, dim):
    return lax.broadcasted_iota(jnp.int32, shape, dim)


def split2(value):
    high = value.astype(BF16)
    low = (value - high.astype(F32)).astype(BF16)
    return high, low


def window_rows(rows, count):
    def add(a, b):
        return b if a is None else (a if b is None else a + b)

    def at(series, i):
        return series.get(i)

    base = {i: rows[i] for i in range(count)}
    two = {i: add(at(base, i), at(base, i + 1)) for i in range(-RIM, count)}
    four = {i: add(at(two, i), at(two, i + 2)) for i in range(-RIM, count)}
    eight = {i: add(at(four, i), at(four, i + 4)) for i in range(-RIM, count)}
    return [add(at(eight, r - RIM), at(base, r + RIM)) for r in range(count)]


def column_band():
    source = lax.rem(iota2((2 * LANES, LANES), 0), LANES)
    return (jnp.abs(source - iota2((2 * LANES, LANES), 1)) <= RIM).astype(BF16)


def edge_matrix(row_count):
    size = row_count * EDGE
    source, target = iota2((size, size), 0), iota2((size, size), 1)
    near = jnp.abs(source // EDGE - target // EDGE) <= RIM
    e, t = source % EDGE, target % EDGE
    left = (e < RIM) & (t >= RIM) & (e >= t - RIM)
    right = (e >= RIM) & (t < RIM) & (t >= e - RIM)
    return (near & (left | right)).astype(BF16)


def observe_kernel(
    row_count, unit_count,
    blocks_ref, weight_ref, edge_weight_ref, band_ref, edge_ref, solve_ref, coord_ref,
    series_ref, sums_ref,
    re_s, im_s, wre_s, wim_s, pw_s, hre_s, him_s, hwre_s, hwim_s, obs_s,
):
    slots = (unit_count + 3) * SUB
    halves = row_count // HALF
    sources = blocks_ref.shape[0]
    per_unit = sources // unit_count
    date_dev = SUB // per_unit
    hbase = 2 * date_dev * row_count
    pad = series_ref.shape[0] // solve_ref.shape[0] * 2

    def place(group, new):
        for s in range(per_unit):
            source = group * per_unit + s
            for d in range(date_dev):
                for c, dst in ((0, re_s), (1, im_s)):
                    start = (d * 2 + c) * row_count
                    values = blocks_ref[source, pl.ds(start, row_count), :].astype(F32)
                    for g in range(row_count // SUB):
                        at = pl.ds(g * SUB * slots + new + s * date_dev + d, SUB, stride=slots)
                        dst[at, :] = values[g * SUB : (g + 1) * SUB]
            edge = blocks_ref[source, pl.ds(hbase, 2 * halves * date_dev), :].astype(F32)
            for c, dst in ((0, hre_s), (1, him_s)):
                for h in range(halves):
                    start = (c * halves + h) * date_dev
                    dst[pl.ds(h * slots + new + s * date_dev, date_dev), :] = edge[start : start + date_dev]

    lane = iota2((SUB, LANES), 1)
    at_edge = (lane >= LANES - RIM) | (lane < RIM)

    def power(re, im, wre, wim, weights, count, new):
        out = []
        for r in range(count):
            at = pl.ds(r * slots + new, SUB)
            w = weights[pl.ds(r, 1), :]
            a_re, a_im = re[at, :], im[at, :]
            w_re, w_im = w * a_re, w * a_im
            wre[at, :] = w_re
            wim[at, :] = w_im
            out.append(w_re * a_re + w_im * a_im)
        return out

    def cross(re, im, wre, wim, count, lag, old):
        out = []
        for r in range(count):
            at, ahead = pl.ds(r * slots + old, SUB), pl.ds(r * slots + old + lag, SUB)
            out.append(wim[at, :] * re[ahead, :] - wre[at, :] * im[ahead, :])
        return out

    def at_edges(images):
        halo = jnp.concatenate([jnp.concatenate(image, axis=1) for image in images], axis=0)
        summed = jnp.dot(jnp.concatenate(split2(halo), axis=0), edge_ref[...], preferred_element_type=F32)
        return summed[: halo.shape[0]] + summed[halo.shape[0] :]

    def look(image, edges):
        rows = jnp.concatenate(window_rows(image, row_count), axis=0)
        summed = jnp.dot(jnp.concatenate(split2(rows), axis=1), band_ref[...], preferred_element_type=F32)
        out = []
        for r in range(row_count):
            tile = edges[:, (r // HALF) * LANES : (r // HALF + 1) * LANES]
            rolled = pltpu.roll(tile, (LANES - RIM - EDGE * (r % HALF)) % LANES, 1)
            out.append(summed[r * SUB : (r + 1) * SUB] + jnp.where(at_edge, rolled, 0.0))
        return out

    def bring(group, new):
        place(lax.rem(group, unit_count), new)
        edges = at_edges([power(hre_s, him_s, hwre_s, hwim_s, edge_weight_ref, halves, new)])
        image = power(re_s, im_s, wre_s, wim_s, weight_ref, row_count, new)
        for r, value in enumerate(look(image, edges)):
            pw_s[pl.ds(r * slots + new, SUB), :] = value

    combos = unit_count * SUB * LAGS

    together = 9 if (unit_count + 1) % 9 == 0 else 3

    def bring_some(step, carry):
        for g in range(together):
            bring(together * step + g, pl.multiple_of((together * step + g) * SUB, SUB))
        return carry

    lax.fori_loop(0, -(-(unit_count + 1) // together), bring_some, 0)

    def observe_unit(unit, carry):
        old = pl.multiple_of(unit * SUB, SUB)
        edges = at_edges([cross(hre_s, him_s, hwre_s, hwim_s, halves, lag, old) for lag in range(1, LAGS + 1)])

        def observed(lag):
            image = cross(re_s, im_s, wre_s, wim_s, row_count, lag, old)
            out = []
            for r, value in enumerate(look(image, edges[(lag - 1) * SUB : lag * SUB])):
                p = pw_s[pl.ds(r * slots + old, SUB), :]
                q = pw_s[pl.ds(r * slots + old + lag, SUB), :]
                out.append(value * lax.rsqrt(p * q + 1e-06))
            return out

        for lag in range(1, LAGS + 1, 2):
            first, second = observed(lag), observed(lag + 1)
            for r in range(row_count):
                at = pl.multiple_of(r * combos + unit * (SUB * LAGS) + (lag - 1) * SUB, 2 * SUB)
                obs_s[pl.ds(at, 2 * SUB), :] = jnp.concatenate([first[r], second[r]], axis=0).astype(BF16)
        return carry

    lax.fori_loop(0, unit_count, observe_unit, 0)

    solve = solve_ref[...]
    date_total = solve.shape[0] // 2
    mean = jnp.zeros((date_total, LANES), F32)
    for r in range(0, row_count, 2):
        pair = [obs_s[pl.ds((r + i) * combos, combos), :] for i in range(2)]
        both = jnp.dot(solve, jnp.concatenate(pair, axis=1), preferred_element_type=F32)
        both = both[:date_total] + both[date_total:]
        for i in range(2):
            series = both[:, i * LANES : (i + 1) * LANES]
            for g in range(date_total // SUB):
                at = pl.ds(g * SUB * pad + r + i, SUB, stride=pad)
                series_ref[at, :] = series[g * SUB : (g + 1) * SUB]
            mean = mean + series
    eye = iota2((date_total, date_total), 0) == iota2((date_total, date_total), 1)
    for i, part in enumerate((mean, mean * coord_ref[...])):
        column = jnp.sum(part, axis=1, keepdims=True)
        sums_ref[pl.ds(i, 1), :] = jnp.sum(jnp.where(eye, column, 0.0), axis=0, keepdims=True)


def observe_all(blocks, weight, edge_weight, solve, coord, row_count, date_dev):
    per_unit = SUB // date_dev
    sources, block_rows, _ = blocks.shape
    unit_count = sources // per_unit
    date_total = unit_count * SUB
    combos = date_total * LAGS
    halves = row_count // HALF
    slots = (unit_count + 3) * SUB
    pad = row_count + SUB
    band, edge = column_band(), edge_matrix(row_count)
    scratch = [pltpu.VMEM((row_count * slots, LANES), F32)] * 5
    scratch += [pltpu.VMEM((halves * slots, LANES), F32)] * 4
    scratch += [pltpu.VMEM((row_count * combos, LANES), BF16)]
    words = row_count * LANES * (5 * slots + combos // 2 + 3 * date_total) + date_total * LANES * combos // 64
    return pl.pallas_call(
        functools.partial(observe_kernel, row_count, unit_count),
        out_shape=(
            jax.ShapeDtypeStruct((date_total * pad, LANES), F32),
            jax.ShapeDtypeStruct((2, date_total), F32),
        ),
        in_specs=[pl.BlockSpec(memory_space=pltpu.VMEM)] * 7,
        out_specs=[pl.BlockSpec(memory_space=pltpu.VMEM)] * 2,
        scratch_shapes=scratch,
        compiler_params=pltpu.CompilerParams(vmem_limit_bytes=min(4 * words + 2**23, 2**26 - 2**17)),
        name="observe",
    )(blocks, weight, edge_weight, band, edge, solve, coord)


def pack_kernel(date_dev, row_count, tiles_ref, out_ref, tiles_s, copies_s, edge_s, in_sems, out_sems, edge_sem):
    strips = out_ref.shape[0]
    size, col_total = tiles_s.shape
    halves = row_count // HALF
    chunks = in_sems.shape[0]
    arrivals = []
    for i in range(chunks):
        at = pl.ds(i * (size // chunks), size // chunks)
        arrivals.append(pltpu.make_async_copy(tiles_ref.at[at], tiles_s.at[at], in_sems.at[i]))
        arrivals[-1].start()
    source, lane = iota2((2 * LANES, LANES), 0), iota2((2 * LANES, LANES), 1) % EDGE
    spread = (lane == jnp.where(source < LANES, source - (LANES - RIM), source - LANES + RIM)) & (
        (source >= LANES) == (lane >= RIM)
    )
    spread = spread.astype(BF16)
    mask = iota2((size, LANES), 0) % HALF == iota2((size, LANES), 1) // EDGE
    out_rows = 2 * halves * date_dev
    target, row = iota2((out_rows, size), 0), iota2((out_rows, size), 1)
    same = (
        (target % date_dev == row // (2 * row_count))
        & (target // (halves * date_dev) == row // row_count % 2)
        & (target // date_dev % halves == row // HALF % halves)
    ).astype(BF16)
    nothing = jnp.zeros((size, LANES), BF16)
    for arrival in arrivals:
        arrival.wait()
    departures = []
    for j in range(strips):
        strip = tiles_s.at[:, pl.ds(j * LANES, LANES)]
        departures.append(pltpu.make_async_copy(strip, out_ref.at[j, pl.ds(0, size)], out_sems.at[j]))
        departures[-1].start()
    for j in range(strips):
        before = tiles_s[:, (j - 1) * LANES : j * LANES] if j else nothing
        after = tiles_s[:, (j + 1) * LANES : (j + 2) * LANES] if j + 1 < strips else nothing
        copies = jnp.dot(jnp.concatenate([before, after], axis=1), spread, preferred_element_type=F32)
        copies_s[:, j * LANES : (j + 1) * LANES] = jnp.where(mask, copies, 0.0).astype(BF16)
    edge = jnp.dot(same, copies_s[...], preferred_element_type=F32).astype(BF16)
    for j in range(strips):
        edge_s[j] = edge[:, j * LANES : (j + 1) * LANES]
    departures.append(pltpu.make_async_copy(edge_s, out_ref.at[:, pl.ds(size, out_rows)], edge_sem.at[0]))
    departures[-1].start()
    for departure in departures:
        departure.wait()


def pack(tiles, devices):
    date_dev, _, row_count, col_total = tiles.shape
    size = date_dev * 2 * row_count
    block_rows = size + 2 * (row_count // HALF) * date_dev
    return pl.pallas_call(
        functools.partial(pack_kernel, date_dev, row_count),
        out_shape=jax.ShapeDtypeStruct((devices, block_rows, LANES), BF16),
        in_specs=[pl.BlockSpec(memory_space=pl.ANY)],
        out_specs=pl.BlockSpec(memory_space=pl.ANY),
        scratch_shapes=[
            pltpu.VMEM((size, col_total), BF16),
            pltpu.VMEM((size, col_total), BF16),
            pltpu.VMEM((devices, block_rows - size, LANES), BF16),
            pltpu.SemaphoreType.DMA((4,)),
            pltpu.SemaphoreType.DMA((devices,)),
            pltpu.SemaphoreType.DMA((1,)),
        ],
        name="pack",
    )(tiles.reshape(size, col_total))


def remove_kernel(pixels, square_sum, series_ref, sums_ref, more_ref, coord_ref, out_ref, out_s, sems):
    dates = sums_ref.shape[1]
    eye = iota2((dates, dates), 0) == iota2((dates, dates), 1)
    sums = sums_ref[...]
    for i in range(more_ref.shape[0]):
        sums = sums + more_ref[i]
    mean = jnp.sum(jnp.where(eye, sums[0:1], 0.0), axis=1, keepdims=True) / pixels
    slope = jnp.sum(jnp.where(eye, sums[1:2], 0.0), axis=1, keepdims=True) / square_sum
    trend = mean + slope * coord_ref[...]
    pad, rows = series_ref.shape[0] // dates, out_ref.shape[0] // dates
    chunks = sems.shape[0]
    per_chunk = dates // chunks
    copies = []
    for i in range(chunks):
        for d in range(i * per_chunk, (i + 1) * per_chunk):
            out_s[pl.ds(d * rows, rows), :] = series_ref[pl.ds(d * pad, rows), :] - trend[d : d + 1]
        at = pl.ds(i * per_chunk * rows, per_chunk * rows)
        copies.append(pltpu.make_async_copy(out_s.at[at], out_ref.at[at], sems.at[i]))
        copies[-1].start()
    for copy in copies:
        copy.wait()


def remove_trend(series, sums, more, coord, rows, pixels, square_sum):
    chunks = 4
    return pl.pallas_call(
        functools.partial(remove_kernel, pixels, square_sum),
        out_shape=jax.ShapeDtypeStruct((rows, LANES), F32),
        in_specs=[pl.BlockSpec(memory_space=pltpu.VMEM)] * 4,
        out_specs=pl.BlockSpec(memory_space=pl.ANY),
        scratch_shapes=[pltpu.VMEM((rows, LANES), F32), pltpu.SemaphoreType.DMA((chunks,))],
        compiler_params=pltpu.CompilerParams(vmem_limit_bytes=8 * series.size + 2**22),
        name="remove",
    )(series, sums, more, coord)


def solve_matrix(pair_list, date_total):
    first, lag = pair_list[:, 0], pair_list[:, 1] - pair_list[:, 0]
    dates = lax.iota(jnp.int32, date_total)
    at_first = (dates[:, None] == first[None, :]).astype(F32)
    at_second = (dates[:, None] == pair_list[None, :, 1]).astype(F32)
    incidence = (at_first - at_second).astype(BF16)
    normal_matrix = jnp.dot(incidence, incidence.T, preferred_element_type=F32) + jnp.eye(date_total, dtype=F32)
    factor = jnp.linalg.cholesky(normal_matrix)
    lags = lax.iota(jnp.int32, LAGS) + 1
    at_lag = (lags[:, None] == lag[None, :]).astype(BF16)
    count = jnp.dot(at_lag, at_first.astype(BF16).T, preferred_element_type=F32)
    second = dates[None, :] + lags[:, None]
    ends = (dates[:, None, None] == dates[None, None, :]).astype(F32) - (
        dates[:, None, None] == second[None]
    ).astype(F32)
    columns = ends * count[None]
    units = date_total // SUB
    columns = columns.reshape(date_total, LAGS, units, SUB).transpose(0, 2, 1, 3).reshape(date_total, LAGS * date_total)
    solved = jax.scipy.linalg.cho_solve((factor, True), columns)
    return jnp.concatenate(split2(solved), axis=0)


def body(slc_tiles, look_weight, pair_list):
    devices = lax.axis_size("gx")
    position = lax.axis_index("gx")
    date_dev, _, row_count, col_total = slc_tiles.shape
    strip = col_total // devices
    date_total = date_dev * devices
    halves = row_count // HALF

    blocks = lax.all_to_all(pack(slc_tiles, devices), "gx", 0, 0, tiled=True)

    weight = lax.dynamic_slice_in_dim(look_weight, position * strip, strip, 1)
    weight_pad = jnp.pad(look_weight, ((0, 0), (RIM, RIM)))
    edge_weight = jnp.concatenate(
        [
            lax.dynamic_slice_in_dim(weight_pad, position * strip, RIM, 1),
            lax.dynamic_slice_in_dim(weight_pad, position * strip + strip + RIM, RIM, 1),
        ],
        axis=1,
    ).reshape(halves, LANES)
    solve = solve_matrix(pair_list, date_total)
    column_ids = position * strip + lax.iota(jnp.int32, strip)
    columns = (2.0 * column_ids.astype(F32) + 1.0) / col_total - 1.0

    series, sums = observe_all(blocks, weight, edge_weight, solve, columns[None], row_count, date_dev)
    rounds = []
    step = devices
    while step > 1:
        width = 4 if step % 4 == 0 else 2
        step //= width
        rounds.append([step * k for k in range(1, width)])
    for i, round_ in enumerate(rounds):
        parts = [lax.ppermute(sums, "gx", [(s, s ^ k) for s in range(devices)]) for k in round_]
        if i + 1 < len(rounds):
            for part in parts:
                sums = sums + part
    square_sum = row_count * (col_total * col_total - 1) / (3 * col_total)
    rows = date_total * row_count
    out = remove_trend(series, sums, jnp.stack(parts), columns[None], rows, float(row_count * col_total), square_sum)
    return out.reshape(date_total, row_count, strip)


def solution(mesh):
    return jax.shard_map(
        body,
        mesh=mesh,
        in_specs=(P("gx", None, "band", None), P("band", None), P()),
        out_specs=P(None, "band", "gx"),
        check_vma=False,
    )
```
